256 devices in a mesh: modes: 32 (over z_lo, y, core), dom: 8 (over x, z_hi).
Axes of the slice: x: 4, y: 4, z: 8 (z_hi: 2, z_lo: 4; z = z_hi * 4 + z_lo), core: 2. Of those that a mesh axis runs over, the one named last changes fastest.
Arguments:
- velocity: float32 [3, 512, 81, 1024], P(None, 'modes', None, 'dom'), may hold values from -6 to 6
- slot_of_cell: int32 [8, 128], P('dom'), may hold values from 0 to 127, each once within a row
- elem_mats: float32 [4, 81, 81], replicated, may hold values from -0.625 to 0.625
- geometry: float32 [4, 1024], P(None, 'dom'), may hold values from 0.5 to 2
Outputs:
- result: float32 [3, 512, 81, 1024], P(None, 'modes', None, 'dom')
The draws below stay inside these ranges and needn't reach their ends.
Inputs may be any that keep to these rules, and one draw needn't show every extreme that they name: `slot_of_cell`: each row is a permutation of the slots 0 to 127.
All inputs are finite; a program needn't handle non-finite values.
Results may differ from the reference program's by a relative error of at most 0.0003.
Values sent between devices are 32-bit elements; how exact they have to be, the bound alone decides.
A program may use at most 128 MiB of HBM per device.

```python
import math
import jax
import jax.numpy as jnp
from jax import lax

EX = 16
EY = 8
ELEMS_DEV = 128
PARTS_SIZE = 8
ELEMS = 1024
PLANES = 512


def shard_levels(key, extent, split, least, largest):
    level = 1.0
    for position, blocks in split:
        draws = jax.random.uniform(jax.random.fold_in(jax.random.fold_in(key, 6), position), (blocks,), jnp.float32, least / len(split), largest / len(split))
        level = level * jnp.repeat(jnp.exp(draws), extent[position] // blocks).reshape((-1,) + (1,) * (len(extent) - 1 - position))
    return level


def bell_draw(own_key, extent, spread, most, shards=(), kind=jnp.bfloat16):
    gain = shard_levels(own_key, extent, shards, -0.22, 0.18) if shards else 1.0
    result = jax.random.normal(own_key, extent, jnp.float32) * spread * gain
    return jnp.minimum(jnp.maximum(result, -most), most).astype(kind)


def setup_inputs(seed: int = 0) -> dict:
    arg_keys = jax.random.split(jax.random.key(seed), 5)
    velocity = bell_draw(arg_keys[0], (3, PLANES, 81, ELEMS), 1.0, 6.0, ((1, 32), (3, 8)), jnp.float32)
    slot_of_cell = jax.vmap(lambda own: jax.random.permutation(own, ELEMS_DEV))(jax.random.split(arg_keys[1], PARTS_SIZE)).reshape((PARTS_SIZE, ELEMS_DEV)).astype(jnp.int32)
    elem_mats = bell_draw(arg_keys[2], (4, 81, 81), 81 ** -0.5, 0.625, (), jnp.float32)
    geometry = jnp.clip(jnp.exp(math.log(2.0) - 1.3862944 * jax.random.uniform(arg_keys[3], (4, ELEMS), jnp.float32) ** shard_levels(arg_keys[3], (4, ELEMS), ((1, 8),), -0.2, 0.2)), 0.5, 2.0)
    return dict(velocity=velocity, slot_of_cell=slot_of_cell, elem_mats=elem_mats, geometry=geometry)


def tables(length):
    indices = jnp.arange(length, dtype=jnp.int32)
    halfway = length // 2
    wavenum = jnp.where(indices <= halfway, indices, indices - halfway)
    phases = (wavenum[:, None] * indices[None, :]) % length
    angles = phases.astype(jnp.float32) * jnp.float32(2.0 * math.pi / length)
    forward = jnp.where((indices <= halfway)[:, None], jnp.cos(angles), jnp.sin(angles))
    weights = jnp.where((indices == 0) | (indices == halfway), jnp.float32(1.0 / length), jnp.float32(2.0 / length))
    inverse = (forward * weights[:, None]).T
    helm_shift = 1.0 + (8.0 * wavenum.astype(jnp.float32) / length) ** 2
    return forward, inverse, helm_shift


def invert(order):
    return jnp.zeros_like(order).at[order].set(jnp.arange(order.shape[0], dtype=jnp.int32))


def assemble(values, slot_of_cell):
    planes = values.shape[0]
    parts = slot_of_cell.shape[0]
    per_part = slot_of_cell.shape[1]
    shaped = values.reshape(planes, 81, parts, per_part)
    picked = jnp.take_along_axis(shaped, slot_of_cell[None, None], axis=3)
    cells_grid = picked.reshape(planes, 9, 9, parts * EX, EY)
    along = cells_grid[:, 8] + jnp.roll(cells_grid[:, 0], -1, axis=2)
    cells_grid = cells_grid.at[:, 8].set(along).at[:, 0].set(jnp.roll(along, 1, axis=2))
    across = cells_grid[:, :, 8, :, :-1] + cells_grid[:, :, 0, :, 1:]
    cells_grid = cells_grid.at[:, :, 8, :, :-1].set(across).at[:, :, 0, :, 1:].set(across)
    flat = cells_grid.reshape(planes, 81, parts, per_part)
    inverse_slot = jax.vmap(invert)(slot_of_cell)
    restored = jnp.take_along_axis(flat, inverse_slot[None, None], axis=3)
    return restored.reshape(planes, 81, parts * per_part)


def reference(velocity, slot_of_cell, elem_mats, geometry):
    forward, inverse, helm_shift = tables(PLANES)

    def component(index):
        product = velocity[index] * velocity[(index + 1) % 3]
        spectra = jnp.einsum('mp,pne->mne', forward, product, precision=lax.Precision.HIGHEST)
        images = jnp.einsum('tij,mje->tmie', elem_mats, spectra, precision=lax.Precision.HIGHEST)
        stiff = images[0] * geometry[0] + images[1] * geometry[1] + images[2] * geometry[2]
        applied = stiff + helm_shift[:, None, None] * (images[3] * geometry[3])
        summed = assemble(applied, slot_of_cell)
        return jnp.einsum('pm,mne->pne', inverse, summed, precision=lax.Precision.HIGHEST)

    return lax.map(component, jnp.arange(3, dtype=jnp.int32))
```

```python
import functools

import jax
import jax.numpy as jnp
import numpy as np
from jax import lax
from jax.experimental import pallas as pl
from jax.experimental.pallas import tpu as pltpu
from jax.sharding import PartitionSpec as P

MESH = pl.DeviceIdType.MESH
F32, BF16 = jnp.float32, jnp.bfloat16
VMEM = pl.BlockSpec(memory_space=pltpu.VMEM)
LANES = 128
EY = 8
ROWS = 64
TALL = 88


def node_order():
    main = [9 * i + j for i in range(8) for j in range(8)]
    return main + [72 + j for j in range(8)] + [9 * i + 8 for i in range(8)] + [80]


def coupling(length):
    index = np.arange(length)
    half = length // 2
    wave = np.where(index <= half, index, index - half)
    angle = 2.0 * np.pi * ((wave[:, None] * index[None, :]) % length) / length
    table = np.where((index <= half)[:, None], np.cos(angle), np.sin(angle))
    weight = np.where((index == 0) | (index == half), 1.0, 2.0) / length
    scale = weight * (8.0 * wave / length) ** 2
    return (table.T * scale) @ table


def halves(x):
    high = x.astype(BF16)
    return high, (x - high.astype(F32)).astype(BF16)


def lane_row(shape=(8, LANES)):
    return lax.broadcasted_iota(jnp.int32, shape, 1), lax.broadcasted_iota(jnp.int32, shape, 0)


def assemble_own(tall):
    lane, row = lane_row()
    block = [tall[8 * i : 8 * i + 8] for i in range(8)]
    right, top, corner = tall[64:72], tall[72:80], tall[80:88]
    inner, upper = lane >= EY, lane % EY >= 1
    top = top + jnp.where(inner, pltpu.roll(corner, EY, 1), 0.0)
    block[0] = block[0] + jnp.where(inner, pltpu.roll(right, EY, 1), 0.0)
    right = right + jnp.where(upper, pltpu.roll(corner, 1, 1), 0.0)
    shifted = jnp.where(upper, pltpu.roll(top, 1, 1), 0.0)
    for i in range(8):
        block[i] = block[i] + jnp.where(row == 0, shifted[i : i + 1], 0.0)
    edge = jnp.where(lane % EY == row, pltpu.roll(top, LANES - 7, 1, stride=1, stride_axis=0), 0.0)
    own = lane // EY == row
    face = jnp.where(own, pltpu.roll(right, EY, 1, stride=EY, stride_axis=0), 0.0)
    face = face + jnp.where(lane == 64, pltpu.roll(corner, 65, 1), 0.0)
    left = jnp.where(own, pltpu.roll(block[0], 0, 1, stride=EY, stride_axis=0), 0.0)
    left = left + jnp.where((lane == 64) & (row == 0), pltpu.roll(top, 57, 1), 0.0)
    total = lambda x: jnp.sum(x, axis=0, keepdims=True)
    return jnp.concatenate(block, axis=0), total(edge), total(face), total(left)


def pre_kernel(depth, slot_ref, geo_ref, mats_ref, vel_ref, w_ref, we_ref, wl_ref, v_ref, ve_ref, vl_ref):
    slots = jnp.broadcast_to(slot_ref[0:1, :], (80, LANES))
    geo = jnp.take_along_axis(geo_ref[...], slots[0:8], axis=1)
    geo = [jnp.broadcast_to(geo[t : t + 1], (TALL, LANES)) for t in range(4)]
    mats = mats_ref[...]
    row16 = lax.broadcasted_iota(jnp.int32, (16, LANES), 0)

    def columns(c, p):
        def product(lo, size):
            part = lambda m: vel_ref[pl.ds((m * 81 + lo) * depth + p, size, stride=depth), :]
            return jnp.take_along_axis(part(c) * part((c + 1) % 3), slots[0:size], axis=1)

        high, low = halves(product(0, 80))
        last = product(73, 8)[7:8]
        last_high = last.astype(BF16).astype(F32)
        rest = jnp.where(row16 < 2, last_high, jnp.where(row16 == 2, last - last_high, 0.0))
        return jnp.concatenate([high, high, low, rest.astype(BF16)], axis=0)

    def pair(step, _):
        for c in range(3):
            rhs = jnp.concatenate([columns(c, 2 * step), columns(c, 2 * step + 1)], axis=1)
            image = jnp.dot(mats, rhs, preferred_element_type=F32)
            for h in range(2):
                part = image[:, LANES * h : LANES * h + LANES]
                terms = [part[TALL * t : TALL * t + TALL] * geo[t] for t in range(4)]
                mass, full = terms[3], (terms[0] + terms[1]) + (terms[2] + terms[3])
                p = 2 * step + h
                for value, r_ref, e_ref, l_ref in ((mass, w_ref, we_ref, wl_ref), (full, v_ref, ve_ref, vl_ref)):
                    rows, edge, face, left = assemble_own(value)
                    r_ref[pl.ds(c * ROWS * depth + p, ROWS, stride=depth), :] = rows
                    e_ref[0, c, pl.ds(p, 1), :] = edge
                    e_ref[1, c, pl.ds(p, 1), :] = face
                    l_ref[c, pl.ds(p, 1), :] = left
        return 0

    lax.fori_loop(0, depth // 2, pair, 0)


def pre(velocity, slots, geometry, mats, depth):
    shapes = [(3 * ROWS * depth, LANES), (2, 3, depth, LANES), (3, depth, LANES)] * 2
    return pl.pallas_call(
        functools.partial(pre_kernel, depth),
        in_specs=[VMEM] * 4,
        out_specs=[VMEM] * 6,
        out_shape=[jax.ShapeDtypeStruct(s, F32) for s in shapes],
        name="pre",
    )(slots, geometry, mats, velocity)


def homes(count):
    return [8, 19, 13, 22, 3, 28] if count == 32 else list(range(6))


def exchange_kernel(
    count, doms, chi_ref, clo_ref, w_ref, we_ref, wl_ref, ve_ref, vl_ref,
    q_ref, qe_ref, gl_ref, gr_ref,
    x, xe, back, backe, first, edges, from_left, from_right,
    send1, recv1, send2, recv2, send_e, recv_e, send_f, recv_f, local,
):
    per = ROWS // count
    early = max(8 // per, 1)
    me, dom = lax.axis_index("modes"), lax.axis_index("dom")
    right, left = lax.rem(dom + 1, doms), lax.rem(dom + doms - 1, doms)
    home = homes(count)

    def remote(src, dst, send, recv, modes, where):
        return pltpu.make_async_remote_copy(
            src_ref=src, dst_ref=dst, send_sem=send, recv_sem=recv, device_id=(modes, where), device_id_type=MESH
        )

    barrier = pltpu.get_barrier_semaphore()

    def greet(k, _):
        pl.semaphore_signal(barrier, inc=1, device_id=(lax.rem(me + k, count), dom), device_id_type=MESH)
        return 0

    for other in (left, right):
        pl.semaphore_signal(barrier, inc=1, device_id=(me, other), device_id_type=MESH)
    lax.fori_loop(1, count, greet, 0)
    pl.semaphore_wait(barrier, count + 1)

    faces = [
        remote(wl_ref, from_right, send_f.at[0], recv_f.at[0], me, left),
        remote(we_ref.at[1], from_left, send_f.at[1], recv_f.at[1], me, right),
    ]
    vfaces = [
        remote(vl_ref, gl_ref, send_f.at[2], recv_f.at[2], me, left),
        remote(ve_ref.at[1], gr_ref, send_f.at[3], recv_f.at[3], me, right),
    ]
    for copy in faces:
        copy.start()

    def bulk(c):
        def step(k, _):
            d = lax.rem(me + k, count)

            @pl.when(d >= early)
            def _():
                remote(w_ref.at[c, d], x.at[c, me], send1.at[c], recv1.at[c], d, dom).start()

            return 0

        lax.fori_loop(1, count, step, 0)

    def late(c):
        for d in range(early):
            @pl.when(me != d)
            def _():
                remote(first.at[c, d], x.at[c, me], send1.at[c], recv1.at[c], d, dom).start()

    bulk(0)
    for copy in vfaces:
        copy.start()
    for copy in faces:
        copy.wait()

    lane = lax.broadcasted_iota(jnp.int32, (16, LANES), 1)
    for c in range(3):
        add = from_left[c]
        for j in range(8):
            piece = jnp.where(lane < EY, pltpu.roll(add, (LANES - EY * j) % LANES, 1), 0.0)
            first[c, j // per, j % per] = w_ref[c, j // per, j % per] + piece
        for r in range(8, early * per):
            first[c, r // per, r % per] = w_ref[c, r // per, r % per]
        edges[c, 0] = we_ref[0, c] + jnp.where(lane == 0, pltpu.roll(add, 64, 1), 0.0)
        edges[c, 1] = we_ref[1, c] + from_right[c]

    late(0)
    for c in range(1, 3):
        bulk(c)
        late(c)
    for k in range(6):
        @pl.when(me != home[k])
        def _():
            remote(edges.at[k // 2, k % 2], xe.at[me], send_e.at[k], recv_e.at[6], home[k], dom).start()

    def apply(value):
        high, low = halves(value)
        chi, clo = chi_ref[...], clo_ref[...]
        dot = functools.partial(jnp.dot, preferred_element_type=F32)
        return dot(chi, high) + (dot(clo, high) + dot(chi, low))

    length = 16 * count

    @pl.when(me < early)
    def _():
        for c in range(3):
            x[c, me] = first[c, jnp.minimum(me, early - 1)]

    @pl.when(me >= early)
    def _():
        for c in range(3):
            x[c, me] = w_ref[c, me]

    for c in range(3):
        pltpu.make_async_copy(x.at[c, pl.ds(0, count - 1)], x.at[c, pl.ds(0, count - 1)], recv1.at[c]).wait()
        for h in range(0, per, 2):
            value = jnp.concatenate([x[c, :, h + i].reshape(length, LANES) for i in range(2)], axis=1)
            value = apply(value)
            for i in range(2):
                back[c, :, h + i] = value[:, LANES * i : LANES * i + LANES].reshape(count, 16, LANES)

        def step(k, _):
            s = lax.rem(me + k, count)
            remote(back.at[c, s], q_ref.at[c, me], send2.at[c], recv2.at[c], s, dom).start()
            return 0

        lax.fori_loop(1, count, step, 0)

    for k in range(6):
        @pl.when(me == home[k])
        def _():
            xe[me] = edges[k // 2, k % 2]
            pltpu.make_async_copy(xe.at[pl.ds(0, count - 1)], xe.at[pl.ds(0, count - 1)], recv_e.at[6]).wait()
            backe[...] = apply(xe[...].reshape(length, LANES)).reshape(count, 16, LANES)
            qe_ref[k // 2, k % 2] = backe[me]

            def step(n, _):
                s = lax.rem(me + n, count)
                remote(backe.at[s], qe_ref.at[k // 2, k % 2], send_e.at[6], recv_e.at[k], s, dom).start()
                return 0

            lax.fori_loop(1, count, step, 0)

    for c in range(3):
        q_ref[c, me] = back[c, me]

    def drain(sem, ref):
        pltpu.make_async_copy(ref, ref, sem).wait()

    for c in range(3):
        drain(send1.at[c], x.at[c, pl.ds(0, count - 1)])
        drain(send2.at[c], x.at[c, pl.ds(0, count - 1)])
        drain(recv2.at[c], q_ref.at[c, pl.ds(0, count - 1)])
    for k in range(6):
        @pl.when(me != home[k])
        def _():
            drain(send_e.at[k], edges.at[0, 0])
            drain(recv_e.at[k], edges.at[0, 0])

        @pl.when(me == home[k])
        def _():
            drain(send_e.at[6], xe.at[pl.ds(0, count - 1)])
    for copy in vfaces:
        copy.wait()


def exchange(chi, clo, w, we, wl, ve, vl):
    count, doms = lax.axis_size("modes"), lax.axis_size("dom")
    per = ROWS // count
    early = max(8 // per, 1)
    depth = wl.shape[1]
    block = (per, depth, LANES)
    return pl.pallas_call(
        functools.partial(exchange_kernel, count, doms),
        in_specs=[VMEM] * 7,
        out_specs=[VMEM] * 4,
        out_shape=[
            jax.ShapeDtypeStruct((3, count) + block, F32),
            jax.ShapeDtypeStruct((3, 2, depth, LANES), F32),
            jax.ShapeDtypeStruct((3, depth, LANES), F32),
            jax.ShapeDtypeStruct((3, depth, LANES), F32),
        ],
        scratch_shapes=[
            pltpu.VMEM((3, count) + block, F32),
            pltpu.VMEM((count, depth, LANES), F32),
            pltpu.VMEM((3, count) + block, F32),
            pltpu.VMEM((count, depth, LANES), F32),
            pltpu.VMEM((3, early) + block, F32),
            pltpu.VMEM((3, 2, depth, LANES), F32),
            pltpu.VMEM((3, depth, LANES), F32),
            pltpu.VMEM((3, depth, LANES), F32),
            pltpu.SemaphoreType.DMA((3,)),
            pltpu.SemaphoreType.DMA((3,)),
            pltpu.SemaphoreType.DMA((3,)),
            pltpu.SemaphoreType.DMA((3,)),
            pltpu.SemaphoreType.DMA((7,)),
            pltpu.SemaphoreType.DMA((7,)),
            pltpu.SemaphoreType.DMA((4,)),
            pltpu.SemaphoreType.DMA((4,)),
            pltpu.SemaphoreType.DMA,
        ],
        compiler_params=pltpu.CompilerParams(collective_id=0, has_side_effects=True),
        name="exchange",
    )(chi, clo, w, we, wl, ve, vl)


def post_kernel(slot_ref, q_ref, qe_ref, v_ref, ve_ref, gl_ref, gr_ref, out_ref):
    depth = out_ref.shape[2]
    square = lax.broadcasted_iota(jnp.int32, (LANES, LANES), 0)
    hot = (jnp.broadcast_to(slot_ref[0:1, :], (LANES, LANES)) == square).astype(BF16)
    index = lax.broadcasted_iota(jnp.int32, (depth, LANES), 1).astype(F32).astype(BF16)
    inverse = lax.dot_general(index, hot, (((1,), (1,)), ((), ())), preferred_element_type=F32).astype(jnp.int32)
    lane = lax.broadcasted_iota(jnp.int32, (depth, LANES), 1)
    inner, lower = lane < LANES - EY, lane % EY < 7

    def put(n, value):
        out_ref[0, n] = jnp.take_along_axis(value, inverse, axis=1)

    turn = lambda value, shift: pltpu.roll(value, shift % LANES, 1)
    came = gr_ref[0]
    edge = ve_ref[0, 0] + qe_ref[0, 0] + jnp.where(lane == 0, turn(came, 64), 0.0)
    face = ve_ref[1, 0] + qe_ref[0, 1] + gl_ref[0]
    row = lambda i, j: v_ref[0, 8 * i + j] + q_ref[0, 8 * i + j]
    for i in range(8):
        for j in range(8):
            value = row(i, j)
            if i == 0:
                value = value + jnp.where(lane < EY, turn(came, -EY * j), 0.0)
                far = jnp.where(inner, turn(value, -EY), turn(face, LANES - EY - EY * j))
                put(72 + j, far)
            if j == 0:
                top = jnp.where(lower, turn(value, -1), turn(edge, 7 - i))
                put(9 * i + 8, top)
                if i == 0:
                    corner = jnp.where(inner, turn(top, -EY), turn(face, 63))
                    put(80, jnp.where(lower, turn(far, -1), corner))
            put(9 * i + j, value)


def post(slots, q, qe, v, ve, gl, gr):
    depth = gl.shape[1]
    rows = pl.BlockSpec((1, ROWS, depth, LANES), lambda c: (c, 0, 0, 0))
    face = pl.BlockSpec((1, depth, LANES), lambda c: (c, 0, 0))
    return pl.pallas_call(
        post_kernel,
        grid=(3,),
        in_specs=[
            pl.BlockSpec((8, LANES), lambda c: (0, 0)),
            rows,
            pl.BlockSpec((1, 2, depth, LANES), lambda c: (c, 0, 0, 0)),
            rows,
            pl.BlockSpec((2, 1, depth, LANES), lambda c: (0, c, 0, 0)),
            face,
            face,
        ],
        out_specs=pl.BlockSpec((1, 81, depth, LANES), lambda c: (c, 0, 0, 0)),
        out_shape=jax.ShapeDtypeStruct((3, 81, depth, LANES), F32),
        name="post",
    )(slots, q, qe, v, ve, gl, gr)


def stacked(elem_mats):
    order = np.array(node_order())
    mats = jnp.pad(elem_mats[:, order, :], ((0, 0), (0, TALL - 81), (0, 0))).reshape(4 * TALL, 81)
    top = lax.reduce_precision(mats, 8, 7)
    high, low = top.astype(BF16), (mats - top).astype(BF16)
    ends = [high[:, 80:], low[:, 80:], high[:, 80:]]
    return jnp.concatenate([high[:, :80], low[:, :80], high[:, :80]] + ends + [jnp.zeros((4 * TALL, 13), BF16)], axis=1)


def body(velocity, slot_of_cell, elem_mats, geometry):
    count = lax.axis_size("modes")
    depth = velocity.shape[1]
    table = coupling(depth * count)
    chi = np.asarray(table, np.float32).astype(jnp.bfloat16)
    clo = (table - chi.astype(np.float64)).astype(np.float32).astype(jnp.bfloat16)
    slots = jnp.broadcast_to(slot_of_cell, (8, LANES))
    geo = jnp.concatenate([geometry, geometry], axis=0)
    flat = jnp.swapaxes(velocity, 1, 2).reshape(3 * 81 * depth, LANES)
    w, we, wl, v, ve, vl = pre(flat, slots, geo, stacked(elem_mats), depth)
    w = w.reshape(3, count, ROWS // count, depth, LANES)
    q, qe, gl, gr = exchange(jnp.asarray(chi), jnp.asarray(clo), w, we, wl, ve, vl)
    result = post(slots, q.reshape(3, ROWS, depth, LANES), qe, v.reshape(3, ROWS, depth, LANES), ve, gl, gr)
    return jnp.swapaxes(result, 1, 2)


def solution(mesh):
    in_specs = (P(None, "modes", None, "dom"), P("dom", None), P(), P(None, "dom"))
    out_specs = P(None, "modes", None, "dom")
    return jax.shard_map(body, mesh=mesh, in_specs=in_specs, out_specs=out_specs, check_vma=False)
```

```python
import functools

import jax
import jax.numpy as jnp
import numpy as np
from jax import lax
from jax.experimental import pallas as pl
from jax.experimental.pallas import tpu as pltpu
from jax.sharding import PartitionSpec as P

MESH = pl.DeviceIdType.MESH
F32, BF16 = jnp.float32, jnp.bfloat16
LANES = 128
EY = 8
ROWS = 64
NODES = 81
TALL = 88


def coupling(length):
    index = np.arange(length)
    half = length // 2
    wave = np.where(index <= half, index, index - half)
    angle = 2.0 * np.pi * ((wave[:, None] * index[None, :]) % length) / length
    table = np.where((index <= half)[:, None], np.cos(angle), np.sin(angle))
    weight = np.where((index == 0) | (index == half), 1.0, 2.0) / length
    scale = weight * (8.0 * wave / length) ** 2
    return (table.T * scale) @ table


def halves(x):
    high = x.astype(BF16)
    return high, (x - high.astype(F32)).astype(BF16)


def turn(value, shift):
    shift = shift % LANES
    return pltpu.roll(value, shift, 1) if shift else value


def homes(count):
    return [8, 19, 13, 22, 3, 28] if count == 32 else list(range(6))


def kernel(
    count, doms, depth,
    slot_ref, geo_ref, mats_ref, chi_hbm, clo_hbm, vel_hbm, out_hbm,
    vel, chi, clo, stage, lhs, rhs, tall,
    w, we, v, ve, x, xe, back, backe, q, qe, to_left, to_right, from_left, from_right, out,
    load, send1, recv1, send2, recv2, send_e, recv_e, send_f, recv_f, store,
):
    half = ROWS // 2 // count
    length = depth * count
    me, dom = lax.axis_index("modes"), lax.axis_index("dom")
    after, before = lax.rem(dom + 1, doms), lax.rem(dom + doms - 1, doms)
    home = homes(count)
    far = [2, 1, 3, 0] if count == 32 else list(range(count // 8))

    def remote(src, dst, send, recv, modes, where):
        return pltpu.make_async_remote_copy(
            src_ref=src, dst_ref=dst, send_sem=send, recv_sem=recv, device_id=(modes, where), device_id_type=MESH
        )

    def drain(sem, ref):
        pltpu.make_async_copy(ref, ref, sem).wait()

    def peers(act):
        def some(low, _):
            for high in far:
                z = lax.rem(me // 8 + high, len(far))
                d = z * 8 + lax.rem(lax.rem(me, 8) + low, 8)
                if high:
                    act(d)
                else:
                    pl.when(low > 0)(lambda: act(d))
            return 0

        lax.fori_loop(0, 8, some, 0)

    loads = [pltpu.make_async_copy(vel_hbm.at[c], vel.at[c], load.at[c]) for c in range(3)]
    loads += [pltpu.make_async_copy(chi_hbm, chi, load.at[3]), pltpu.make_async_copy(clo_hbm, clo, load.at[4])]
    for copy in loads:
        copy.start()
    barrier = pltpu.get_barrier_semaphore()
    for other in (before, after):
        pl.semaphore_signal(barrier, inc=1, device_id=(me, other), device_id_type=MESH)
    peers(lambda d: pl.semaphore_signal(barrier, inc=1, device_id=(d, dom), device_id_type=MESH))

    wide = lax.broadcasted_iota(jnp.int32, (TALL, LANES), 1)

    def stack(t):
        stage[...] = jnp.zeros_like(stage)
        for i in range(8):
            stage[8 * i : 8 * i + 8, 0:NODES] = mats_ref[t, 9 * i : 9 * i + 8, :]
            stage[72 + i : 73 + i, 0:NODES] = mats_ref[t, 9 * i + 8 : 9 * i + 9, :]
        stage[64:72, 0:NODES] = mats_ref[t, 72:80, :]
        stage[80:81, 0:NODES] = mats_ref[t, 80:81, :]
        full = stage[...]
        high = full.astype(BF16).astype(F32)
        low = full - high
        low_turned = turn(low, 80)
        first = jnp.where(wide < 80, high, low_turned)
        second = jnp.where(wide < 32, low_turned, turn(high, 32))
        second = jnp.where(wide == 113, turn(low, 33), jnp.where(wide == 114, turn(high, 34), second))
        second = jnp.where(wide < 115, second, 0.0)
        lhs[TALL * t : TALL * t + TALL, 0:LANES] = first.astype(BF16)
        lhs[TALL * t : TALL * t + TALL, LANES:] = second.astype(BF16)

    stack(3)
    slots = jnp.broadcast_to(slot_ref[0:1, :], (80, LANES))
    geo = [
        jnp.take_along_axis(jnp.broadcast_to(geo_ref[t : t + 1, :], (8, LANES)), slots[0:8], axis=1)[0:1] for t in range(4)
    ]
    row16 = lax.broadcasted_iota(jnp.int32, (16, LANES), 0)
    lane = lax.broadcasted_iota(jnp.int32, (depth, LANES), 1)
    inner, upper = lane >= EY, lane % EY >= 1

    def columns(c, p):
        def product(lo, size):
            part = lambda m: vel[m, pl.ds(lo * depth + p, size, stride=depth), :]
            return jnp.take_along_axis(part(c) * part(lax.rem(c + 1, 3)), slots[0:size], axis=1)

        high, low = halves(product(0, 80))
        last = product(73, 8)[7:8]
        last_high = last.astype(BF16).astype(F32)
        rest = jnp.where(row16 < 2, last_high, jnp.where(row16 == 2, last - last_high, 0.0))
        return jnp.concatenate([high, high, low, rest.astype(BF16)], axis=0)

    def assemble(rows, ends):
        at = lambda r: tall[r * depth : r * depth + depth, :]
        corner = at(80)
        edge = jnp.zeros((depth, LANES), F32)
        face = jnp.where(lane == 64, turn(corner, 65), 0.0)
        for i in range(8):
            top = at(72 + i)
            if i == 0:
                top = top + jnp.where(inner, turn(corner, EY), 0.0)
            edge = jnp.where(lane % EY == i, turn(top, i - 7), edge)
            for j in range(8):
                value = at(8 * i + j)
                if i == 0:
                    value = value + jnp.where(inner, turn(at(64 + j), EY), 0.0)
                if j == 0:
                    value = value + jnp.where(upper, turn(top, 1), 0.0)
                rows(8 * i + j, value)
        for j in range(8):
            right = at(64 + j)
            if j == 0:
                right = right + jnp.where(upper, turn(corner, 1), 0.0)
            face = jnp.where(lane // EY == j, turn(right, EY + EY * j), face)
        ends(edge, face)

    def mass(c):
        scale = jnp.broadcast_to(geo[3], (TALL, LANES))

        def pair(step, _):
            block = jnp.concatenate([columns(c, 2 * step), columns(c, 2 * step + 1)], axis=1)
            rhs[c * (depth // 2) + step] = block
            image = jnp.dot(lhs[3 * TALL :, :], block, preferred_element_type=F32)
            for h in range(2):
                tall[pl.ds(2 * step + h, TALL, stride=depth), :] = image[:, LANES * h : LANES * h + LANES] * scale
            return 0

        lax.fori_loop(0, depth // 2, pair, 0, unroll=2)

        def rows(r, value):
            w[c, r // (half * count) , r % (half * count) // half, r % half] = value

        def ends(edge, face):
            we[2 * c], we[2 * c + 1] = edge, face

        assemble(rows, ends)

    def stiff(c):
        scale = [jnp.broadcast_to(g, (TALL, LANES)) for g in geo]

        def pair(step, _):
            image = jnp.dot(lhs[...], rhs[c * (depth // 2) + step], preferred_element_type=F32)
            for h in range(2):
                part = image[:, LANES * h : LANES * h + LANES]
                terms = [part[TALL * t : TALL * t + TALL] * scale[t] for t in range(4)]
                tall[pl.ds(2 * step + h, TALL, stride=depth), :] = (terms[0] + terms[1]) + (terms[2] + terms[3])
            return 0

        lax.fori_loop(0, depth // 2, pair, 0, unroll=2)

        def rows(r, value):
            v[c, r] = value

        def ends(edge, face):
            ve[2 * c], ve[2 * c + 1] = edge, face

        assemble(rows, ends)

    def send_both(c):
        peers(lambda d: remote(w.at[c, :, d], x.at[c, :, me], send1.at[c], recv1.at[c], d, dom).start())

    def send_half(h):
        peers(lambda d: remote(w.at[2, h, d], x.at[2, h, me], send1.at[2 + h], recv1.at[2 + h], d, dom).start())

    def send_ends(c):
        for k in range(2):
            for n in range(3):
                @pl.when((c == n) & (me != home[2 * n + k]))
                def _():
                    e = 2 * n + k
                    remote(we.at[e], xe.at[me], send_e.at[e], recv_e.at[6], home[e], dom).start()

    loads[0].wait()
    loads[1].wait()
    mass(0)
    pl.semaphore_wait(barrier, count + 1)
    send_both(0)
    send_ends(0)
    loads[2].wait()

    def others(c, _):
        mass(c)

        @pl.when(c == 1)
        def _():
            send_both(1)

        send_ends(c)
        return 0

    lax.fori_loop(1, 3, others, 0)
    send_half(0)
    send_half(1)
    for t in range(3):
        stack(t)

    def stiffs(c, _):
        stiff(c)
        return 0

    lax.fori_loop(0, 3, stiffs, 0)

    loads[3].wait()
    loads[4].wait()

    def apply(value):
        high, low = halves(value)
        dot = functools.partial(jnp.dot, preferred_element_type=F32)
        return dot(chi[...], high) + (dot(clo[...], high) + dot(chi[...], low))

    for c in range(2):
        for h in range(2):
            x[c, h, me] = w[c, h, me]
    for h in range(2):
        x[2, h, me] = w[2, h, me]

    def transform(c, h):
        places = [(0, r) for r in range(half)] + [(1, r) for r in range(half)] if h is None else [(h, r) for r in range(half)]
        for n in range(0, len(places), 2):
            two = places[n : n + 2]
            value = apply(jnp.concatenate([x[c, a, :, r].reshape(length, LANES) for a, r in two], axis=1))
            for k, (a, r) in enumerate(two):
                back[c, a, :, r] = value[:, LANES * k : LANES * k + LANES].reshape(count, depth, LANES)

    for c in range(2):
        drain(recv1.at[c], x.at[c, :, pl.ds(0, count - 1)])
        transform(c, None)
        peers(lambda s: remote(back.at[c, :, s], q.at[c, :, me], send2.at[c], recv2.at[c], s, dom).start())

    for e in range(6):
        @pl.when(me == home[e])
        def _():
            xe[me] = we[e]
            drain(recv_e.at[6], xe.at[pl.ds(0, count - 1)])
            backe[...] = apply(xe[...].reshape(length, LANES)).reshape(count, depth, LANES)
            qe[e] = backe[me]
            peers(lambda s: remote(backe.at[s], qe.at[e], send_e.at[6], recv_e.at[e], s, dom).start())

    for h in range(2):
        drain(recv1.at[2 + h], x.at[2, h, pl.ds(0, count - 1)])
        transform(2, h)
        peers(lambda s: remote(back.at[2, h, s], q.at[2, h, me], send2.at[2 + h], recv2.at[2 + h], s, dom).start())
    for c in range(3):
        for h in range(2):
            q[c, h, me] = back[c, h, me]

    square = lax.broadcasted_iota(jnp.int32, (LANES, LANES), 0)
    hot = (jnp.broadcast_to(slot_ref[0:1, :], (LANES, LANES)) == square).astype(BF16)
    index = lane.astype(F32).astype(BF16)
    inverse = lax.dot_general(index, hot, (((1,), (1,)), ((), ())), preferred_element_type=F32).astype(jnp.int32)
    below, lower = lane < LANES - EY, lane % EY < 7

    def row(c, r):
        return v[c, r] + q[c, r // (half * count), r % (half * count) // half, r % half]

    def faces(c):
        return [
            remote(to_left.at[c], from_right.at[c], send_f.at[2 * c], recv_f.at[2 * c], me, before),
            remote(to_right.at[c], from_left.at[c], send_f.at[2 * c + 1], recv_f.at[2 * c + 1], me, after),
        ]

    def send_faces(c):
        for k in range(2):
            e = 2 * c + k
            pl.when(me != home[e])(lambda: drain(recv_e.at[e], qe.at[0]))
            ve[e] = ve[e] + qe[e]
        value = turn(ve[2 * c], 64)
        for j in range(8):
            value = jnp.where(lane // EY == j, turn(row(c, j), EY * j), value)
        to_left[c] = value
        to_right[c] = ve[2 * c + 1]
        for copy in faces(c):
            copy.start()

    def expand(c, low, high):
        def put(n, value):
            out[c, n] = jnp.take_along_axis(value, inverse, axis=1)

        came = from_left[c]
        edge = ve[2 * c] + jnp.where(lane == 0, turn(came, 64), 0.0)
        if low == 0:
            face = ve[2 * c + 1] + from_right[c]
        for i in range(low, high):
            for j in range(8):
                value = row(c, 8 * i + j)
                if i == 0:
                    value = value + jnp.where(lane < EY, turn(came, -EY * j), 0.0)
                    right = jnp.where(below, turn(value, -EY), turn(face, LANES - EY - EY * j))
                    put(72 + j, right)
                if j == 0:
                    top = jnp.where(lower, turn(value, -1), turn(edge, 7 - i))
                    put(9 * i + 8, top)
                    if i == 0:
                        corner = jnp.where(below, turn(top, -EY), turn(face, 63))
                        put(80, jnp.where(lower, turn(right, -1), corner))
                put(9 * i + j, value)

    stores = [pltpu.make_async_copy(out.at[c], out_hbm.at[c], store.at[c]) for c in range(2)]
    stores.append(pltpu.make_async_copy(out.at[2, 0:36], out_hbm.at[2, 0:36], store.at[2]))
    stores.append(pltpu.make_async_copy(out.at[2, 72:], out_hbm.at[2, 72:], store.at[3]))
    stores.append(pltpu.make_async_copy(out.at[2, 36:72], out_hbm.at[2, 36:72], store.at[4]))
    rest = pl.ds(0, count - 1)
    for c in range(2):
        drain(recv2.at[c], q.at[c, :, rest])
        send_faces(c)
    for c in range(2):
        for copy in faces(c):
            copy.wait()
        expand(c, 0, 8)
        stores[c].start()
    drain(recv2.at[2], q.at[2, 0, rest])
    send_faces(2)
    for copy in faces(2):
        copy.wait()
    expand(2, 0, 4)
    stores[2].start()
    stores[3].start()
    drain(recv2.at[3], q.at[2, 1, rest])
    expand(2, 4, 8)
    stores[4].start()

    for c in range(2):
        drain(send1.at[c], x.at[c, :, rest])
        drain(send2.at[c], x.at[c, :, rest])
        drain(send1.at[2 + c], x.at[2, 0, rest])
        drain(send2.at[2 + c], x.at[2, 0, rest])
    for e in range(6):
        pl.when(me != home[e])(lambda: drain(send_e.at[e], we.at[0]))
        pl.when(me == home[e])(lambda: drain(send_e.at[6], xe.at[rest]))
    for copy in stores:
        copy.wait()


def step(slots, geometry, mats, chi, clo, velocity):
    count, doms = lax.axis_size("modes"), lax.axis_size("dom")
    depth = velocity.shape[1] // NODES
    half = ROWS // 2 // count
    wire = (3, 2, count, half, depth, LANES)
    ends = (6, depth, LANES)
    single = (count, depth, LANES)
    face = (3, depth, LANES)
    vmem, dma = pltpu.VMEM, pltpu.SemaphoreType.DMA
    here, there = pl.BlockSpec(memory_space=pltpu.VMEM), pl.BlockSpec(memory_space=pl.ANY)
    return pl.pallas_call(
        functools.partial(kernel, count, doms, depth),
        in_specs=[here] * 3 + [there] * 3,
        out_specs=there,
        out_shape=jax.ShapeDtypeStruct((3, NODES, depth, LANES), F32),
        scratch_shapes=[
            vmem((3, NODES * depth, LANES), F32),
            vmem(chi.shape, BF16),
            vmem(clo.shape, BF16),
            vmem((TALL, LANES), F32),
            vmem((4 * TALL, 2 * LANES), BF16),
            vmem((3 * depth // 2, 256, 2 * LANES), BF16),
            vmem((TALL * depth, LANES), F32),
            vmem(wire, F32),
            vmem(ends, F32),
            vmem((3, ROWS, depth, LANES), F32),
            vmem(ends, F32),
            vmem(wire, F32),
            vmem(single, F32),
            vmem(wire, F32),
            vmem(single, F32),
            vmem(wire, F32),
            vmem(ends, F32),
            vmem(face, F32),
            vmem(face, F32),
            vmem(face, F32),
            vmem(face, F32),
            vmem((3, NODES, depth, LANES), F32),
            dma((5,)),
            dma((4,)),
            dma((4,)),
            dma((4,)),
            dma((4,)),
            dma((7,)),
            dma((7,)),
            dma((6,)),
            dma((6,)),
            dma((5,)),
        ],
        compiler_params=pltpu.CompilerParams(collective_id=0, has_side_effects=True),
        name="step",
    )(slots, geometry, mats, chi, clo, velocity)


def body(velocity, slot_of_cell, elem_mats, geometry):
    depth = velocity.shape[1]
    table = coupling(depth * lax.axis_size("modes"))
    chi = np.asarray(table, np.float32).astype(jnp.bfloat16)
    clo = (table - chi.astype(np.float64)).astype(np.float32).astype(jnp.bfloat16)
    flat = jnp.swapaxes(velocity, 1, 2).reshape(3, NODES * depth, LANES)
    result = step(slot_of_cell, geometry, elem_mats, jnp.asarray(chi), jnp.asarray(clo), flat)
    return jnp.swapaxes(result, 1, 2)


def solution(mesh):
    in_specs = (P(None, "modes", None, "dom"), P("dom", None), P(), P(None, "dom"))
    out_specs = P(None, "modes", None, "dom")
    return jax.shard_map(body, mesh=mesh, in_specs=in_specs, out_specs=out_specs, check_vma=False)
```

```python
import functools

import jax
import jax.numpy as jnp
import numpy as np
from jax import lax
from jax.experimental import pallas as pl
from jax.experimental.pallas import tpu as pltpu
from jax.sharding import PartitionSpec as P

MESH = pl.DeviceIdType.MESH
F32, BF16 = jnp.float32, jnp.bfloat16
LANES = 128
EY = 8
ROWS = 64
NODES = 81
TALL = 88


def coupling(length):
    index = np.arange(length)
    half = length // 2
    wave = np.where(index <= half, index, index - half)
    angle = 2.0 * np.pi * ((wave[:, None] * index[None, :]) % length) / length
    table = np.where((index <= half)[:, None], np.cos(angle), np.sin(angle))
    weight = np.where((index == 0) | (index == half), 1.0, 2.0) / length
    scale = weight * (8.0 * wave / length) ** 2
    return (table.T * scale) @ table


def halves(x):
    high = x.astype(BF16)
    return high, (x - high.astype(F32)).astype(BF16)


def turn(value, shift):
    shift = shift % LANES
    return pltpu.roll(value, shift, 1) if shift else value


def homes(count):
    return [8, 19, 13, 22, 3, 28] if count == 32 else list(range(6))


def place(c, i, j):
    if i == 0:
        return 8 * c + j
    if c == 0:
        return 24 + 8 * i + j
    if c == 1:
        return 80 + 8 * i + j
    return (30 + j if j < 2 else 190 + j) if i == 7 else 136 + 8 * i + j


def kernel(
    count, doms, depth,
    slot_hbm, geo_hbm, mats_hbm, chi_hbm, clo_hbm, vel_hbm, out_hbm,
    slot_ref, geo_ref, mats_ref, vel, chi, clo, stage, lhs, rhs, tall,
    w, we, v, ve, x, xe, back, backe, q, qe, to_left, to_right, from_left, from_right, out,
    load, send1, recv1, send2, recv2, send_e, recv_e, send_f, recv_f, store,
):
    unit = 32 // count
    chunks = [(0, 1), (1, 2), (2, 3), (3, 5), (5, 6)]
    spans = [(unit * a, unit * (b - a)) for a, b in chunks]
    length = depth * count
    me, dom = lax.axis_index("modes"), lax.axis_index("dom")
    after, before = lax.rem(dom + 1, doms), lax.rem(dom + doms - 1, doms)
    home = homes(count)
    far = [2, 1, 3, 0] if count == 32 else list(range(count // 8))

    def remote(src, dst, send, recv, modes, where):
        return pltpu.make_async_remote_copy(
            src_ref=src, dst_ref=dst, send_sem=send, recv_sem=recv, device_id=(modes, where), device_id_type=MESH
        )

    def drain(sem, ref):
        pltpu.make_async_copy(ref, ref, sem).wait()

    def peers(act):
        def some(low, _):
            for high in far:
                z = lax.rem(me // 8 + high, len(far))
                d = z * 8 + lax.rem(lax.rem(me, 8) + low, 8)
                if high:
                    act(d)
                else:
                    pl.when(low > 0)(lambda: act(d))
            return 0

        lax.fori_loop(0, 8, some, 0)

    loads = [pltpu.make_async_copy(vel_hbm.at[c], vel.at[c], load.at[c]) for c in range(3)]
    loads += [pltpu.make_async_copy(chi_hbm, chi, load.at[3]), pltpu.make_async_copy(clo_hbm, clo, load.at[4])]
    small = ((slot_hbm, slot_ref), (geo_hbm, geo_ref), (mats_hbm, mats_ref))
    loads += [pltpu.make_async_copy(src, dst, load.at[5 + n]) for n, (src, dst) in enumerate(small)]
    barrier = pltpu.get_barrier_semaphore()
    for other in (before, after):
        pl.semaphore_signal(barrier, inc=1, device_id=(me, other), device_id_type=MESH)
    peers(lambda d: pl.semaphore_signal(barrier, inc=1, device_id=(d, dom), device_id_type=MESH))
    for n in (7, 5, 6, 0, 1, 2, 3, 4):
        loads[n].start()
    for n in (5, 6, 7):
        loads[n].wait()

    wide = lax.broadcasted_iota(jnp.int32, (TALL, LANES), 1)

    def stack(t):
        stage[...] = jnp.zeros_like(stage)
        for i in range(8):
            stage[8 * i : 8 * i + 8, 0:NODES] = mats_ref[9 * i : 9 * i + 8, t, :]
            stage[72 + i : 73 + i, 0:NODES] = mats_ref[9 * i + 8 : 9 * i + 9, t, :]
        stage[64:72, 0:NODES] = mats_ref[72:80, t, :]
        stage[80:81, 0:NODES] = mats_ref[80:81, t, :]
        full = stage[...]
        high = full.astype(BF16).astype(F32)
        low = full - high
        low_turned = turn(low, 80)
        first = jnp.where(wide < 80, high, low_turned)
        second = jnp.where(wide < 32, low_turned, turn(high, 32))
        second = jnp.where(wide == 113, turn(low, 33), jnp.where(wide == 114, turn(high, 34), second))
        second = jnp.where(wide < 115, second, 0.0)
        lhs[TALL * t : TALL * t + TALL, 0:LANES] = first.astype(BF16)
        lhs[TALL * t : TALL * t + TALL, LANES:] = second.astype(BF16)

    stack(3)
    slots = jnp.broadcast_to(slot_ref[0:1, :], (80, LANES))
    geo = [
        jnp.take_along_axis(jnp.broadcast_to(geo_ref[t : t + 1, :], (8, LANES)), slots[0:8], axis=1)[0:1] for t in range(4)
    ]
    row16 = lax.broadcasted_iota(jnp.int32, (16, LANES), 0)
    lane = lax.broadcasted_iota(jnp.int32, (depth, LANES), 1)
    inner, upper = lane >= EY, lane % EY >= 1

    def columns(c, p):
        def product(lo, size):
            part = lambda m: vel[m, pl.ds(lo * depth + p, size, stride=depth), :]
            return jnp.take_along_axis(part(c) * part((c + 1) % 3), slots[0:size], axis=1)

        high, low = halves(product(0, 80))
        last = product(73, 8)[7:8]
        last_high = last.astype(BF16).astype(F32)
        rest = jnp.where(row16 < 2, last_high, jnp.where(row16 == 2, last - last_high, 0.0))
        return jnp.concatenate([high, high, low, rest.astype(BF16)], axis=0)

    def assemble(rows, ends):
        at = lambda r: tall[r * depth : r * depth + depth, :]
        corner = at(80)
        edge = jnp.zeros((depth, LANES), F32)
        face = jnp.where(lane == 64, turn(corner, 65), 0.0)
        for i in range(8):
            top = at(72 + i)
            if i == 0:
                top = top + jnp.where(inner, turn(corner, EY), 0.0)
            edge = jnp.where(lane % EY == i, turn(top, i - 7), edge)
            for j in range(8):
                value = at(8 * i + j)
                if i == 0:
                    value = value + jnp.where(inner, turn(at(64 + j), EY), 0.0)
                if j == 0:
                    value = value + jnp.where(upper, turn(top, 1), 0.0)
                rows(i, j, value)
        for j in range(8):
            right = at(64 + j)
            if j == 0:
                right = right + jnp.where(upper, turn(corner, 1), 0.0)
            face = jnp.where(lane // EY == j, turn(right, EY + EY * j), face)
        ends(edge, face)

    def mass(c):
        scale = jnp.broadcast_to(geo[3], (TALL, LANES))

        def pair(step, _):
            block = jnp.concatenate([columns(c, 2 * step), columns(c, 2 * step + 1)], axis=1)
            rhs[c * (depth // 2) + step] = block
            image = jnp.dot(lhs[3 * TALL :, :], block, preferred_element_type=F32)
            for h in range(2):
                tall[pl.ds(2 * step + h, TALL, stride=depth), :] = image[:, LANES * h : LANES * h + LANES] * scale
            return 0

        lax.fori_loop(0, depth // 2, pair, 0, unroll=2)

        def rows(i, j, value):
            n = place(c, i, j)
            if n < 192:
                w[n // count, n % count] = value
            else:
                we[n - 192] = value

        def ends(edge, face):
            for k, value in enumerate((edge, face)):
                w[(24 + 2 * c + k) // count, (24 + 2 * c + k) % count] = value

        assemble(rows, ends)

    def stiff(c):
        scale = [jnp.broadcast_to(g, (TALL, LANES)) for g in geo]

        def pair(step, _):
            image = jnp.dot(lhs[...], rhs[c * (depth // 2) + step], preferred_element_type=F32)
            for h in range(2):
                part = image[:, LANES * h : LANES * h + LANES]
                terms = [part[TALL * t : TALL * t + TALL] * scale[t] for t in range(4)]
                tall[pl.ds(2 * step + h, TALL, stride=depth), :] = (terms[0] + terms[1]) + (terms[2] + terms[3])
            return 0

        lax.fori_loop(0, depth // 2, pair, 0, unroll=2)

        def rows(i, j, value):
            v[c, 8 * i + j] = value

        def ends(edge, face):
            ve[2 * c], ve[2 * c + 1] = edge, face

        assemble(rows, ends)

    def go(n):
        a, size = spans[n]
        peers(lambda d: remote(w.at[pl.ds(a, size), d], x.at[pl.ds(a, size), me], send1.at[n], recv1.at[n], d, dom).start())

    def come(n):
        a, size = spans[n]
        peers(lambda s: remote(back.at[pl.ds(a, size), s], q.at[pl.ds(a, size), me], send2.at[n], recv2.at[n], s, dom).start())

    rest = pl.ds(0, count - 1)

    def arrived(sem, ref, n):
        drain(sem.at[n], ref.at[pl.ds(*spans[n]), rest])

    loads[0].wait()
    loads[1].wait()
    mass(0)
    pl.semaphore_wait(barrier, count + 1)
    go(1)
    loads[2].wait()
    mass(1)
    mass(2)
    go(0)
    for e in range(6):
        @pl.when(me != home[e])
        def _():
            remote(we.at[e], xe.at[me], send_e.at[e], recv_e.at[6], home[e], dom).start()
    go(2)
    for t in range(3):
        stack(t)
    for c in range(3):
        stiff(c)
    loads[3].wait()
    loads[4].wait()

    def apply(value):
        high, low = halves(value)
        dot = functools.partial(jnp.dot, preferred_element_type=F32)
        return dot(chi[...], high) + (dot(clo[...], high) + dot(chi[...], low))

    def transform(n):
        a, size = spans[n]
        arrived(recv1, x, n)
        for r in range(a, a + size):
            x[r, me] = w[r, me]
        for r in range(a, a + size, 2):
            two = range(r, min(r + 2, a + size))
            value = apply(jnp.concatenate([x[k].reshape(length, LANES) for k in two], axis=1))
            for m, k in enumerate(two):
                back[k] = value[:, LANES * m : LANES * m + LANES].reshape(count, depth, LANES)
        for r in range(a, a + size):
            q[r, me] = back[r, me]

    square = lax.broadcasted_iota(jnp.int32, (LANES, LANES), 0)
    hot = (jnp.broadcast_to(slot_ref[0:1, :], (LANES, LANES)) == square).astype(BF16)
    index = lane.astype(F32).astype(BF16)
    inverse = lax.dot_general(index, hot, (((1,), (1,)), ((), ())), preferred_element_type=F32).astype(jnp.int32)
    below, lower = lane < LANES - EY, lane % EY < 7
    lane8 = lane[0:8]

    def row(c, i, j):
        n = place(c, i, j)
        return v[c, 8 * i + j] + (q[n // count, n % count] if n < 192 else qe[n - 192])

    faces = [
        remote(to_left, from_right, send_f.at[0], recv_f.at[0], me, before),
        remote(to_right, from_left, send_f.at[1], recv_f.at[1], me, after),
    ]

    def pack(ref, values):
        last = jnp.zeros((8, LANES), F32)
        for c, value in enumerate(values):
            upper_planes, lower_planes = value[0:8], value[8:16]
            ref[c] = jnp.where(lane8 < 64, upper_planes, turn(lower_planes, 64))
            last = jnp.where(lane8 == 2 * c, turn(upper_planes, 64 + 2 * c), last)
            last = jnp.where(lane8 == 2 * c + 1, turn(lower_planes, 65 + 2 * c), last)
        ref[3] = last

    def unpack(ref, c):
        main, last = ref[c], ref[3]
        pick = lambda value, k: jnp.where(lane8 == 64, turn(last, 64 - 2 * c - k), value)
        return jnp.concatenate([pick(main, 0), pick(turn(main, 64), 1)], axis=0)

    def send_faces():
        lefts, rights = [], []
        for c in range(3):
            for k in range(2):
                n = 24 + 2 * c + k
                ve[2 * c + k] = ve[2 * c + k] + q[n // count, n % count]
            value = turn(ve[2 * c], 64)
            for j in range(8):
                value = jnp.where(lane // EY == j, turn(row(c, 0, j), EY * j), value)
            lefts.append(value)
            rights.append(ve[2 * c + 1])
        pack(to_left, lefts)
        pack(to_right, rights)
        for copy in faces:
            copy.start()

    def expand(c, parts):
        def put(n, value):
            out[c, n] = jnp.take_along_axis(value, inverse, axis=1)

        came = unpack(from_left, c)
        edge = ve[2 * c] + jnp.where(lane == 0, turn(came, 64), 0.0)
        if 0 in parts:
            face = ve[2 * c + 1] + unpack(from_right, c)
        for i in parts:
            for j in range(8):
                value = row(c, i, j)
                if i == 0:
                    value = value + jnp.where(lane < EY, turn(came, -EY * j), 0.0)
                    right = jnp.where(below, turn(value, -EY), turn(face, LANES - EY - EY * j))
                    put(72 + j, right)
                if j == 0:
                    top = jnp.where(lower, turn(value, -1), turn(edge, 7 - i))
                    put(9 * i + 8, top)
                    if i == 0:
                        corner = jnp.where(below, turn(top, -EY), turn(face, 63))
                        put(80, jnp.where(lower, turn(right, -1), corner))
                put(9 * i + j, value)

    transform(0)
    come(0)
    go(3)
    go(4)
    transform(1)
    transform(2)
    arrived(recv2, q, 0)
    send_faces()
    come(1)
    come(2)
    for e in range(6):
        @pl.when(me == home[e])
        def _():
            xe[me] = we[e]
            drain(recv_e.at[6], xe.at[rest])
            backe[...] = apply(xe[...].reshape(length, LANES)).reshape(count, depth, LANES)
            qe[e] = backe[me]
            peers(lambda s: remote(backe.at[s], qe.at[e], send_e.at[6], recv_e.at[e], s, dom).start())

    for n in (3, 4):
        transform(n)
        come(n)

    pieces = [(0, 0, 81), (1, 0, 81), (2, 0, 27), (2, 63, 81), (2, 27, 63)]
    stores = [
        pltpu.make_async_copy(out.at[c, a:b], out_hbm.at[c, a:b], store.at[n]) for n, (c, a, b) in enumerate(pieces)
    ]
    arrived(recv2, q, 1)
    arrived(recv2, q, 2)
    for copy in faces:
        copy.wait()
    expand(0, range(8))
    stores[0].start()
    for e in range(6):
        pl.when(me != home[e])(lambda: drain(recv_e.at[e], qe.at[0]))
    arrived(recv2, q, 3)
    expand(1, range(8))
    stores[1].start()
    expand(2, (0, 1, 2, 7))
    stores[2].start()
    stores[3].start()
    arrived(recv2, q, 4)
    expand(2, (3, 4, 5, 6))
    stores[4].start()

    for n in range(5):
        arrived(send1, x, n)
        arrived(send2, x, n)
    for e in range(6):
        pl.when(me != home[e])(lambda: drain(send_e.at[e], we.at[0]))
        pl.when(me == home[e])(lambda: drain(send_e.at[6], xe.at[rest]))
    for copy in stores:
        copy.wait()


def step(slots, geometry, mats, chi, clo, velocity):
    count, doms = lax.axis_size("modes"), lax.axis_size("dom")
    depth = velocity.shape[1] // NODES
    wire = (6 * 32 // count, count, depth, LANES)
    ends = (6, depth, LANES)
    single = (count, depth, LANES)
    face = (4, depth // 2, LANES)
    vmem, dma = pltpu.VMEM, pltpu.SemaphoreType.DMA
    there = pl.BlockSpec(memory_space=pl.ANY)
    return pl.pallas_call(
        functools.partial(kernel, count, doms, depth),
        in_specs=[there] * 6,
        out_specs=there,
        out_shape=jax.ShapeDtypeStruct((3, NODES, depth, LANES), F32),
        scratch_shapes=[
            vmem(slots.shape, jnp.int32),
            vmem(geometry.shape, F32),
            vmem(mats.shape, F32),
            vmem((3, NODES * depth, LANES), F32),
            vmem(chi.shape, BF16),
            vmem(clo.shape, BF16),
            vmem((TALL, LANES), F32),
            vmem((4 * TALL, 2 * LANES), BF16),
            vmem((3 * depth // 2, 256, 2 * LANES), BF16),
            vmem((TALL * depth, LANES), F32),
            vmem(wire, F32),
            vmem(ends, F32),
            vmem((3, ROWS, depth, LANES), F32),
            vmem(ends, F32),
            vmem(wire, F32),
            vmem(single, F32),
            vmem(wire, F32),
            vmem(single, F32),
            vmem(wire, F32),
            vmem(ends, F32),
            vmem(face, F32),
            vmem(face, F32),
            vmem(face, F32),
            vmem(face, F32),
            vmem((3, NODES, depth, LANES), F32),
            dma((8,)),
            dma((5,)),
            dma((5,)),
            dma((5,)),
            dma((5,)),
            dma((7,)),
            dma((7,)),
            dma((2,)),
            dma((2,)),
            dma((5,)),
        ],
        compiler_params=pltpu.CompilerParams(collective_id=0, has_side_effects=True),
        name="step",
    )(slots, geometry, mats, chi, clo, velocity)


def body(velocity, slot_of_cell, elem_mats, geometry):
    depth = velocity.shape[1]
    table = coupling(depth * lax.axis_size("modes"))
    chi = np.asarray(table, np.float32).astype(jnp.bfloat16)
    clo = (table - chi.astype(np.float64)).astype(np.float32).astype(jnp.bfloat16)
    flat = jnp.swapaxes(velocity, 1, 2).reshape(3, NODES * depth, LANES)
    result = step(slot_of_cell, geometry, jnp.swapaxes(elem_mats, 0, 1), jnp.asarray(chi), jnp.asarray(clo), flat)
    return jnp.swapaxes(result, 1, 2)


def solution(mesh):
    in_specs = (P(None, "modes", None, "dom"), P("dom", None), P(), P(None, "dom"))
    out_specs = P(None, "modes", None, "dom")
    return jax.shard_map(body, mesh=mesh, in_specs=in_specs, out_specs=out_specs, check_vma=False)
```

```python
import functools

import jax
import jax.numpy as jnp
import numpy as np
from jax import lax
from jax.experimental import pallas as pl
from jax.experimental.pallas import tpu as pltpu
from jax.sharding import PartitionSpec as P

MESH = pl.DeviceIdType.MESH
F32, BF16 = jnp.float32, jnp.bfloat16
LANES = 128
EY = 8
ROWS = 64
NODES = 81
TALL = 88


def coupling(length):
    index = np.arange(length)
    half = length // 2
    wave = np.where(index <= half, index, index - half)
    angle = 2.0 * np.pi * ((wave[:, None] * index[None, :]) % length) / length
    table = np.where((index <= half)[:, None], np.cos(angle), np.sin(angle))
    weight = np.where((index == 0) | (index == half), 1.0, 2.0) / length
    scale = weight * (8.0 * wave / length) ** 2
    return (table.T * scale) @ table


def halves(x):
    high = x.astype(BF16)
    return high, (x - high.astype(F32)).astype(BF16)


def turn(value, shift):
    shift = shift % LANES
    return pltpu.roll(value, shift, 1) if shift else value


def homes(count):
    return [8, 19, 13, 22, 3, 28] if count == 32 else list(range(6))


def place(c, i, j):
    if i == 0:
        return 8 * c + j
    if c == 0:
        return 24 + 8 * i + j
    if c == 1:
        return 80 + 8 * i + j
    return (30 + j if j < 2 else 190 + j) if i == 7 else 136 + 8 * i + j


def kernel(
    count, doms, depth,
    slot_hbm, geo_hbm, mats_hbm, chi_hbm, clo_hbm, vel_hbm, out,
    slot_ref, geo_ref, mats_ref, vel, chi, clo, stage, lhs, rhs, tall,
    w, we, v, ve, x, xe, back, backe, q, qe, to_left, to_right, from_left, from_right,
    load, send1, recv1, send2, recv2, send_e, recv_e, send_f, recv_f, hello,
):
    unit = 32 // count
    chunks = [(0, 1), (1, 2), (2, 3), (3, 5), (5, 6)]
    spans = [(unit * a, unit * (b - a)) for a, b in chunks]
    length = depth * count
    me, dom = lax.axis_index("modes"), lax.axis_index("dom")
    after, before = lax.rem(dom + 1, doms), lax.rem(dom + doms - 1, doms)
    home = homes(count)
    far = [2, 1, 3, 0] if count == 32 else list(range(count // 8))

    def remote(src, dst, send, recv, modes, where):
        return pltpu.make_async_remote_copy(
            src_ref=src, dst_ref=dst, send_sem=send, recv_sem=recv, device_id=(modes, where), device_id_type=MESH
        )

    def drain(sem, ref):
        pltpu.make_async_copy(ref, ref, sem).wait()

    def peers(act):
        def some(low, _):
            for high in far:
                z = lax.rem(me // 8 + high, len(far))
                d = z * 8 + lax.rem(lax.rem(me, 8) + low, 8)
                if high:
                    act(d)
                else:
                    pl.when(low > 0)(lambda: act(d))
            return 0

        lax.fori_loop(0, 8, some, 0)

    loads = [pltpu.make_async_copy(vel_hbm.at[c], vel.at[c], load.at[c]) for c in range(3)]
    loads += [pltpu.make_async_copy(chi_hbm, chi, load.at[3]), pltpu.make_async_copy(clo_hbm, clo, load.at[4])]
    small = ((slot_hbm, slot_ref), (geo_hbm, geo_ref), (mats_hbm, mats_ref))
    loads += [pltpu.make_async_copy(src, dst, load.at[5 + n]) for n, (src, dst) in enumerate(small)]
    barrier = pltpu.get_barrier_semaphore()
    gate = max(count // 2 - 4, 0)

    @pl.when(me == gate)
    def _():
        for other in (before, after):
            pl.semaphore_signal(barrier, inc=1, device_id=(me, other), device_id_type=MESH)

    peers(lambda d: pl.semaphore_signal(barrier, inc=1, device_id=(d, dom), device_id_type=MESH))
    for n in (7, 5, 6, 0, 1, 2, 3, 4):
        loads[n].start()
    for n in (5, 6, 7):
        loads[n].wait()

    wide = lax.broadcasted_iota(jnp.int32, (TALL, LANES), 1)

    def stack(t):
        stage[...] = jnp.zeros_like(stage)
        for i in range(8):
            stage[8 * i : 8 * i + 8, 0:NODES] = mats_ref[9 * i : 9 * i + 8, t, :]
            stage[72 + i : 73 + i, 0:NODES] = mats_ref[9 * i + 8 : 9 * i + 9, t, :]
        stage[64:72, 0:NODES] = mats_ref[72:80, t, :]
        stage[80:81, 0:NODES] = mats_ref[80:81, t, :]
        full = stage[...]
        high = full.astype(BF16).astype(F32)
        low = full - high
        low_turned = turn(low, 80)
        first = jnp.where(wide < 80, high, low_turned)
        second = jnp.where(wide < 32, low_turned, turn(high, 32))
        second = jnp.where(wide == 113, turn(low, 33), jnp.where(wide == 114, turn(high, 34), second))
        second = jnp.where(wide < 115, second, 0.0)
        lhs[TALL * t : TALL * t + TALL, 0:LANES] = first.astype(BF16)
        lhs[TALL * t : TALL * t + TALL, LANES:] = second.astype(BF16)

    stack(3)
    slots = jnp.broadcast_to(slot_ref[0:1, :], (80, LANES))
    geo = [
        jnp.take_along_axis(jnp.broadcast_to(geo_ref[t : t + 1, :], (8, LANES)), slots[0:8], axis=1)[0:1] for t in range(4)
    ]
    row16 = lax.broadcasted_iota(jnp.int32, (16, LANES), 0)
    lane = lax.broadcasted_iota(jnp.int32, (depth, LANES), 1)
    inner, upper = lane >= EY, lane % EY >= 1

    def columns(c, p):
        def product(lo, size):
            part = lambda m: vel[m, pl.ds(lo * depth + p, size, stride=depth), :]
            return jnp.take_along_axis(part(c) * part((c + 1) % 3), slots[0:size], axis=1)

        high, low = halves(product(0, 80))
        last = product(73, 8)[7:8]
        last_high = last.astype(BF16).astype(F32)
        rest = jnp.where(row16 < 2, last_high, jnp.where(row16 == 2, last - last_high, 0.0))
        return jnp.concatenate([high, high, low, rest.astype(BF16)], axis=0)

    def assemble(rows, ends):
        at = lambda r: tall[r * depth : r * depth + depth, :]
        corner = at(80)
        edge = jnp.zeros((depth, LANES), F32)
        face = jnp.where(lane == 64, turn(corner, 65), 0.0)
        for i in range(8):
            top = at(72 + i)
            if i == 0:
                top = top + jnp.where(inner, turn(corner, EY), 0.0)
            edge = jnp.where(lane % EY == i, turn(top, i - 7), edge)
            for j in range(8):
                value = at(8 * i + j)
                if i == 0:
                    value = value + jnp.where(inner, turn(at(64 + j), EY), 0.0)
                if j == 0:
                    value = value + jnp.where(upper, turn(top, 1), 0.0)
                rows(i, j, value)
        for j in range(8):
            right = at(64 + j)
            if j == 0:
                right = right + jnp.where(upper, turn(corner, 1), 0.0)
            face = jnp.where(lane // EY == j, turn(right, EY + EY * j), face)
        ends(edge, face)

    def mass(c):
        scale = jnp.broadcast_to(geo[3], (TALL, LANES))

        def pair(step, _):
            block = jnp.concatenate([columns(c, 2 * step), columns(c, 2 * step + 1)], axis=1)
            rhs[c * (depth // 2) + step] = block
            image = jnp.dot(lhs[3 * TALL :, :], block, preferred_element_type=F32)
            for h in range(2):
                tall[pl.ds(2 * step + h, TALL, stride=depth), :] = image[:, LANES * h : LANES * h + LANES] * scale
            return 0

        lax.fori_loop(0, depth // 2, pair, 0, unroll=2)

        def rows(i, j, value):
            n = place(c, i, j)
            if n < 192:
                w[n // count, n % count] = value
            else:
                we[n - 192] = value

        def ends(edge, face):
            for k, value in enumerate((edge, face)):
                w[(24 + 2 * c + k) // count, (24 + 2 * c + k) % count] = value

        assemble(rows, ends)

    def stiff(c):
        scale = [jnp.broadcast_to(g, (TALL, LANES)) for g in geo]

        def pair(step, _):
            image = jnp.dot(lhs[...], rhs[c * (depth // 2) + step], preferred_element_type=F32)
            for h in range(2):
                part = image[:, LANES * h : LANES * h + LANES]
                terms = [part[TALL * t : TALL * t + TALL] * scale[t] for t in range(4)]
                tall[pl.ds(2 * step + h, TALL, stride=depth), :] = (terms[0] + terms[1]) + (terms[2] + terms[3])
            return 0

        lax.fori_loop(0, depth // 2, pair, 0, unroll=2)

        def rows(i, j, value):
            v[c, 8 * i + j] = value

        def ends(edge, face):
            ve[2 * c], ve[2 * c + 1] = edge, face

        assemble(rows, ends)

    def go(n):
        a, size = spans[n]
        peers(lambda d: remote(w.at[pl.ds(a, size), d], x.at[pl.ds(a, size), me], send1.at[n], recv1.at[n], d, dom).start())

    def come(n):
        a, size = spans[n]
        peers(lambda s: remote(back.at[pl.ds(a, size), s], q.at[pl.ds(a, size), me], send2.at[n], recv2.at[n], s, dom).start())

    rest = pl.ds(0, count - 1)

    def arrived(sem, ref, n):
        drain(sem.at[n], ref.at[pl.ds(*spans[n]), rest])

    loads[0].wait()
    loads[1].wait()
    mass(0)
    pl.when(me != gate)(lambda: pl.semaphore_wait(barrier, count - 1))
    pl.when(me == gate)(lambda: pl.semaphore_wait(barrier, count + 1))
    go(1)
    loads[2].wait()
    mass(1)
    mass(2)
    go(0)
    for e in range(6):
        @pl.when(me != home[e])
        def _():
            remote(we.at[e], xe.at[me], send_e.at[e], recv_e.at[6], home[e], dom).start()
    go(2)
    for t in range(3):
        stack(t)
    for c in range(3):
        stiff(c)
    loads[3].wait()
    loads[4].wait()

    def apply(value):
        high, low = halves(value)
        dot = functools.partial(jnp.dot, preferred_element_type=F32)
        return dot(chi[...], high) + (dot(clo[...], high) + dot(chi[...], low))

    def transform(n):
        a, size = spans[n]
        arrived(recv1, x, n)
        for r in range(a, a + size):
            x[r, me] = w[r, me]
        for r in range(a, a + size, 2):
            two = range(r, min(r + 2, a + size))
            value = apply(jnp.concatenate([x[k].reshape(length, LANES) for k in two], axis=1))
            for m, k in enumerate(two):
                back[k] = value[:, LANES * m : LANES * m + LANES].reshape(count, depth, LANES)
        for r in range(a, a + size):
            q[r, me] = back[r, me]

    square = lax.broadcasted_iota(jnp.int32, (LANES, LANES), 0)
    hot = (jnp.broadcast_to(slot_ref[0:1, :], (LANES, LANES)) == square).astype(BF16)
    index = lane.astype(F32).astype(BF16)
    inverse = lax.dot_general(index, hot, (((1,), (1,)), ((), ())), preferred_element_type=F32).astype(jnp.int32)
    below, lower = lane < LANES - EY, lane % EY < 7
    lane8 = lane[0:8]

    def row(c, i, j):
        n = place(c, i, j)
        return v[c, 8 * i + j] + (q[n // count, n % count] if n < 192 else qe[n - 192])

    faces = [
        remote(to_left, from_right, send_f.at[0], recv_f.at[0], me, before),
        remote(to_right, from_left, send_f.at[1], recv_f.at[1], me, after),
    ]

    def pack(ref, values):
        last = jnp.zeros((8, LANES), F32)
        for c, value in enumerate(values):
            upper_planes, lower_planes = value[0:8], value[8:16]
            ref[c] = jnp.where(lane8 < 64, upper_planes, turn(lower_planes, 64))
            last = jnp.where(lane8 == 2 * c, turn(upper_planes, 64 + 2 * c), last)
            last = jnp.where(lane8 == 2 * c + 1, turn(lower_planes, 65 + 2 * c), last)
        ref[3] = last

    def unpack(ref, c):
        main, last = ref[c], ref[3]
        pick = lambda value, k: jnp.where(lane8 == 64, turn(last, 64 - 2 * c - k), value)
        return jnp.concatenate([pick(main, 0), pick(turn(main, 64), 1)], axis=0)

    def send_faces():
        lefts, rights = [], []
        for c in range(3):
            for k in range(2):
                n = 24 + 2 * c + k
                ve[2 * c + k] = ve[2 * c + k] + q[n // count, n % count]
            value = turn(ve[2 * c], 64)
            for j in range(8):
                value = jnp.where(lane // EY == j, turn(row(c, 0, j), EY * j), value)
            lefts.append(value)
            rights.append(ve[2 * c + 1])
        pack(to_left, lefts)
        pack(to_right, rights)
        for copy in faces:
            copy.start()

    def expand(c, parts):
        def put(n, value):
            out[c, n] = jnp.take_along_axis(value, inverse, axis=1)

        came = unpack(from_left, c)
        edge = ve[2 * c] + jnp.where(lane == 0, turn(came, 64), 0.0)
        if 0 in parts:
            face = ve[2 * c + 1] + unpack(from_right, c)
        for i in parts:
            for j in range(8):
                value = row(c, i, j)
                if i == 0:
                    value = value + jnp.where(lane < EY, turn(came, -EY * j), 0.0)
                    right = jnp.where(below, turn(value, -EY), turn(face, LANES - EY - EY * j))
                    put(72 + j, right)
                if j == 0:
                    top = jnp.where(lower, turn(value, -1), turn(edge, 7 - i))
                    put(9 * i + 8, top)
                    if i == 0:
                        corner = jnp.where(below, turn(top, -EY), turn(face, 63))
                        put(80, jnp.where(lower, turn(right, -1), corner))
                put(9 * i + j, value)

    @pl.when(me == gate)
    def _():
        for n, other in enumerate((before, after)):
            pl.semaphore_signal(hello.at[n], inc=1, device_id=(me, other), device_id_type=MESH)

    transform(0)
    come(0)
    go(3)
    go(4)

    @pl.when(me == gate)
    def _():
        for n in range(2):
            pl.semaphore_wait(hello.at[n], 1)
        peers(lambda d: pl.semaphore_signal(hello.at[2], inc=1, device_id=(d, dom), device_id_type=MESH))

    transform(1)
    transform(2)
    arrived(recv2, q, 0)
    pl.when(me != gate)(lambda: pl.semaphore_wait(hello.at[2], 1))
    send_faces()
    come(1)
    come(2)
    for e in range(6):
        @pl.when(me == home[e])
        def _():
            xe[me] = we[e]
            drain(recv_e.at[6], xe.at[rest])
            backe[...] = apply(xe[...].reshape(length, LANES)).reshape(count, depth, LANES)
            qe[e] = backe[me]
            peers(lambda s: remote(backe.at[s], qe.at[e], send_e.at[6], recv_e.at[e], s, dom).start())

    for n in (3, 4):
        transform(n)
        come(n)

    arrived(recv2, q, 1)
    arrived(recv2, q, 2)
    for copy in faces:
        copy.wait()
    expand(0, range(8))
    for e in range(6):
        pl.when(me != home[e])(lambda: drain(recv_e.at[e], qe.at[0]))
    arrived(recv2, q, 3)
    expand(1, range(8))
    expand(2, (0, 1, 2, 7))
    arrived(recv2, q, 4)
    expand(2, (3, 4, 5, 6))

    for n in range(5):
        arrived(send1, x, n)
        arrived(send2, x, n)
    for e in range(6):
        pl.when(me != home[e])(lambda: drain(send_e.at[e], we.at[0]))
        pl.when(me == home[e])(lambda: drain(send_e.at[6], xe.at[rest]))


def step(slots, geometry, mats, chi, clo, velocity):
    count, doms = lax.axis_size("modes"), lax.axis_size("dom")
    depth = velocity.shape[1] // NODES
    wire = (6 * 32 // count, count, depth, LANES)
    ends = (6, depth, LANES)
    single = (count, depth, LANES)
    face = (4, depth // 2, LANES)
    vmem, dma = pltpu.VMEM, pltpu.SemaphoreType.DMA
    there = pl.BlockSpec(memory_space=pl.ANY)
    return pl.pallas_call(
        functools.partial(kernel, count, doms, depth),
        in_specs=[there] * 6,
        out_specs=pl.BlockSpec(memory_space=pltpu.VMEM),
        out_shape=pltpu.VMEM((3, NODES, depth, LANES), F32),
        scratch_shapes=[
            vmem(slots.shape, jnp.int32),
            vmem(geometry.shape, F32),
            vmem(mats.shape, F32),
            vmem((3, NODES * depth, LANES), F32),
            vmem(chi.shape, BF16),
            vmem(clo.shape, BF16),
            vmem((TALL, LANES), F32),
            vmem((4 * TALL, 2 * LANES), BF16),
            vmem((3 * depth // 2, 256, 2 * LANES), BF16),
            vmem((TALL * depth, LANES), F32),
            vmem(wire, F32),
            vmem(ends, F32),
            vmem((3, ROWS, depth, LANES), F32),
            vmem(ends, F32),
            vmem(wire, F32),
            vmem(single, F32),
            vmem(wire, F32),
            vmem(single, F32),
            vmem(wire, F32),
            vmem(ends, F32),
            vmem(face, F32),
            vmem(face, F32),
            vmem(face, F32),
            vmem(face, F32),
            dma((8,)),
            dma((5,)),
            dma((5,)),
            dma((5,)),
            dma((5,)),
            dma((7,)),
            dma((7,)),
            dma((2,)),
            dma((2,)),
            pltpu.SemaphoreType.REGULAR((3,)),
        ],
        compiler_params=pltpu.CompilerParams(collective_id=0, has_side_effects=True),
        name="step",
    )(slots, geometry, mats, chi, clo, velocity)


def body(velocity, slot_of_cell, elem_mats, geometry):
    depth = velocity.shape[1]
    table = coupling(depth * lax.axis_size("modes"))
    chi = np.asarray(table, np.float32).astype(jnp.bfloat16)
    clo = (table - chi.astype(np.float64)).astype(np.float32).astype(jnp.bfloat16)
    flat = jnp.swapaxes(velocity, 1, 2).reshape(3, NODES * depth, LANES)
    result = step(slot_of_cell, geometry, jnp.swapaxes(elem_mats, 0, 1), jnp.asarray(chi), jnp.asarray(clo), flat)
    return jnp.swapaxes(result, 1, 2)


def solution(mesh):
    in_specs = (P(None, "modes", None, "dom"), P("dom", None), P(), P(None, "dom"))
    out_specs = P(None, "modes", None, "dom")
    return jax.shard_map(body, mesh=mesh, in_specs=in_specs, out_specs=out_specs, check_vma=False)
```

```python
import functools

import jax
import jax.numpy as jnp
import numpy as np
from jax import lax
from jax.experimental import pallas as pl
from jax.experimental.pallas import tpu as pltpu
from jax.sharding import PartitionSpec as P

MESH = pl.DeviceIdType.MESH
F32, BF16 = jnp.float32, jnp.bfloat16
LANES = 128
EY = 8
ROWS = 64
NODES = 81
TALL = 88


def coupling(length):
    index = np.arange(length)
    half = length // 2
    wave = np.where(index <= half, index, index - half)
    angle = 2.0 * np.pi * ((wave[:, None] * index[None, :]) % length) / length
    table = np.where((index <= half)[:, None], np.cos(angle), np.sin(angle))
    weight = np.where((index == 0) | (index == half), 1.0, 2.0) / length
    scale = weight * (8.0 * wave / length) ** 2
    return (table.T * scale) @ table


def halves(x):
    high = x.astype(BF16)
    return high, (x - high.astype(F32)).astype(BF16)


def turn(value, shift):
    shift = shift % LANES
    return pltpu.roll(value, shift, 1) if shift else value


def homes(count):
    return [8, 19, 13, 22, 3, 28] if count == 32 else list(range(6))


def place(c, i, j):
    if i == 0:
        return 8 * c + j
    if c == 0:
        return 24 + 8 * i + j
    if c == 1:
        return 80 + 8 * i + j
    return (30 + j if j < 2 else 190 + j) if i == 7 else 136 + 8 * i + j


def kernel(
    count, doms, depth,
    slot_hbm, geo_hbm, mats_hbm, chi_hbm, clo_hbm, vel_hbm, out,
    slot_ref, geo_ref, mats_ref, vel, chi, clo, stage, lhs, rhs, tall,
    w, we, v, ve, line, x, xe, back, backe, q, qe, to_left, to_right, from_left, from_right,
    load, send_z, recv_z, send1, recv1, send2, recv2, send_e, recv_e, send_f, recv_f, hello,
):
    unit = 32 // count
    chunks = [(0, 1), (1, 2), (2, 3), (3, 5), (5, 6)]
    spans = [(unit * a, unit * (b - a)) for a, b in chunks]
    length = depth * count
    me, dom = lax.axis_index("modes"), lax.axis_index("dom")
    after, before = lax.rem(dom + 1, doms), lax.rem(dom + doms - 1, doms)
    home = homes(count)
    far = [2, 1, 3, 0] if count == 32 else list(range(count // 8))

    def remote(src, dst, send, recv, modes, where):
        return pltpu.make_async_remote_copy(
            src_ref=src, dst_ref=dst, send_sem=send, recv_sem=recv, device_id=(modes, where), device_id_type=MESH
        )

    def drain(sem, ref):
        pltpu.make_async_copy(ref, ref, sem).wait()

    def peers(act):
        def some(low, _):
            for high in far:
                z = lax.rem(me // 8 + high, len(far))
                d = z * 8 + lax.rem(lax.rem(me, 8) + low, 8)
                if high:
                    act(d)
                else:
                    pl.when(low > 0)(lambda: act(d))
            return 0

        lax.fori_loop(0, 8, some, 0)

    loads = [pltpu.make_async_copy(vel_hbm.at[c], vel.at[c], load.at[c]) for c in range(3)]
    loads += [pltpu.make_async_copy(chi_hbm, chi, load.at[3]), pltpu.make_async_copy(clo_hbm, clo, load.at[4])]
    small = ((slot_hbm, slot_ref), (geo_hbm, geo_ref), (mats_hbm, mats_ref))
    loads += [pltpu.make_async_copy(src, dst, load.at[5 + n]) for n, (src, dst) in enumerate(small)]
    barrier = pltpu.get_barrier_semaphore()
    gate = max(count // 2 - 4, 0)
    planes = count // 8
    zme, yme = me // 8, lax.rem(me, 8)
    line_peers = [lax.rem(zme + high, planes) * 8 + yme for high in range(1, planes)]
    plane_peers = [zme * 8 + lax.rem(yme + low, 8) for low in range(1, 8)]
    heard = planes - 1 + 7

    def signal(sem, modes, where):
        pl.semaphore_signal(sem, inc=1, device_id=(modes, where), device_id_type=MESH)

    for d in line_peers + plane_peers:
        signal(barrier, d, dom)

    @pl.when((yme == gate % 8) & (zme != gate // 8))
    def _():
        signal(barrier, gate + 1, dom)

    @pl.when(me == gate)
    def _():
        for other in (before, after):
            signal(barrier, me, other)

    for n in (7, 5, 6, 0, 1, 2, 3, 4):
        loads[n].start()
    for n in (5, 6, 7):
        loads[n].wait()

    wide = lax.broadcasted_iota(jnp.int32, (TALL, LANES), 1)

    def stack(t):
        stage[...] = jnp.zeros_like(stage)
        for i in range(8):
            stage[8 * i : 8 * i + 8, 0:NODES] = mats_ref[9 * i : 9 * i + 8, t, :]
            stage[72 + i : 73 + i, 0:NODES] = mats_ref[9 * i + 8 : 9 * i + 9, t, :]
        stage[64:72, 0:NODES] = mats_ref[72:80, t, :]
        stage[80:81, 0:NODES] = mats_ref[80:81, t, :]
        full = stage[...]
        high = full.astype(BF16).astype(F32)
        low = full - high
        low_turned = turn(low, 80)
        first = jnp.where(wide < 80, high, low_turned)
        second = jnp.where(wide < 32, low_turned, turn(high, 32))
        second = jnp.where(wide == 113, turn(low, 33), jnp.where(wide == 114, turn(high, 34), second))
        second = jnp.where(wide < 115, second, 0.0)
        lhs[TALL * t : TALL * t + TALL, 0:LANES] = first.astype(BF16)
        lhs[TALL * t : TALL * t + TALL, LANES:] = second.astype(BF16)

    stack(3)
    slots = jnp.broadcast_to(slot_ref[0:1, :], (80, LANES))
    geo = [
        jnp.take_along_axis(jnp.broadcast_to(geo_ref[t : t + 1, :], (8, LANES)), slots[0:8], axis=1)[0:1] for t in range(4)
    ]
    row16 = lax.broadcasted_iota(jnp.int32, (16, LANES), 0)
    lane = lax.broadcasted_iota(jnp.int32, (depth, LANES), 1)
    inner, upper = lane >= EY, lane % EY >= 1

    def columns(c, p):
        def product(lo, size):
            part = lambda m: vel[m, pl.ds(lo * depth + p, size, stride=depth), :]
            return jnp.take_along_axis(part(c) * part((c + 1) % 3), slots[0:size], axis=1)

        high, low = halves(product(0, 80))
        last = product(73, 8)[7:8]
        last_high = last.astype(BF16).astype(F32)
        rest = jnp.where(row16 < 2, last_high, jnp.where(row16 == 2, last - last_high, 0.0))
        return jnp.concatenate([high, high, low, rest.astype(BF16)], axis=0)

    def assemble(rows, ends):
        at = lambda r: tall[r * depth : r * depth + depth, :]
        corner = at(80)
        edge = jnp.zeros((depth, LANES), F32)
        face = jnp.where(lane == 64, turn(corner, 65), 0.0)
        for i in range(8):
            top = at(72 + i)
            if i == 0:
                top = top + jnp.where(inner, turn(corner, EY), 0.0)
            edge = jnp.where(lane % EY == i, turn(top, i - 7), edge)
            for j in range(8):
                value = at(8 * i + j)
                if i == 0:
                    value = value + jnp.where(inner, turn(at(64 + j), EY), 0.0)
                if j == 0:
                    value = value + jnp.where(upper, turn(top, 1), 0.0)
                rows(i, j, value)
        for j in range(8):
            right = at(64 + j)
            if j == 0:
                right = right + jnp.where(upper, turn(corner, 1), 0.0)
            face = jnp.where(lane // EY == j, turn(right, EY + EY * j), face)
        ends(edge, face)

    def mass(c):
        scale = jnp.broadcast_to(geo[3], (TALL, LANES))

        def pair(step, _):
            block = jnp.concatenate([columns(c, 2 * step), columns(c, 2 * step + 1)], axis=1)
            rhs[c * (depth // 2) + step] = block
            image = jnp.dot(lhs[3 * TALL :, :], block, preferred_element_type=F32)
            for h in range(2):
                tall[pl.ds(2 * step + h, TALL, stride=depth), :] = image[:, LANES * h : LANES * h + LANES] * scale
            return 0

        lax.fori_loop(0, depth // 2, pair, 0, unroll=2)

        def rows(i, j, value):
            n = place(c, i, j)
            if n < 192:
                w[n // count, n % count] = value
            else:
                we[n - 192] = value

        def ends(edge, face):
            for k, value in enumerate((edge, face)):
                w[(24 + 2 * c + k) // count, (24 + 2 * c + k) % count] = value

        assemble(rows, ends)

    def stiff(c):
        scale = [jnp.broadcast_to(g, (TALL, LANES)) for g in geo]

        def pair(step, _):
            image = jnp.dot(lhs[...], rhs[c * (depth // 2) + step], preferred_element_type=F32)
            for h in range(2):
                part = image[:, LANES * h : LANES * h + LANES]
                terms = [part[TALL * t : TALL * t + TALL] * scale[t] for t in range(4)]
                tall[pl.ds(2 * step + h, TALL, stride=depth), :] = (terms[0] + terms[1]) + (terms[2] + terms[3])
            return 0

        lax.fori_loop(0, depth // 2, pair, 0, unroll=2)

        def rows(i, j, value):
            v[c, 8 * i + j] = value

        def ends(edge, face):
            ve[2 * c], ve[2 * c + 1] = edge, face

        assemble(rows, ends)

    def go(n):
        a, size = spans[n]
        peers(lambda d: remote(w.at[pl.ds(a, size), d], x.at[pl.ds(a, size), zme, yme], send1.at[n], recv1.at[n], d, dom).start())

    def come(n):
        a, size = spans[n]
        peers(lambda s: remote(back.at[pl.ds(a, size), s], q.at[pl.ds(a, size), me], send2.at[n], recv2.at[n], s, dom).start())

    rest = pl.ds(0, count - 1)

    def arrived(sem, ref, n):
        drain(sem.at[n], ref.at[pl.ds(*spans[n]), rest])

    loads[0].wait()
    loads[1].wait()
    mass(0)
    pl.when((me != gate) & (me != gate + 1))(lambda: pl.semaphore_wait(barrier, heard))
    pl.when(me == gate)(lambda: pl.semaphore_wait(barrier, heard + 2))
    pl.when(me == gate + 1)(lambda: pl.semaphore_wait(barrier, heard + planes - 1))

    @pl.when(me != gate)
    def _():
        for d in plane_peers:
            signal(hello.at[3], d, dom)

    own = pl.ds(unit, unit)
    for d in line_peers:
        block = w.at[own, pl.ds(d - yme, 8)]
        remote(block, line.at[:, zme], send_z.at[0], recv_z.at[0], d, dom).start()
    for k in range(unit):
        for n in range(8):
            line[k, zme, n] = w[unit + k, zme * 8 + n]

    def relay():
        if planes > 1:
            drain(recv_z.at[0], line.at[:, pl.ds(0, planes - 1)])
        for d in plane_peers:
            src, dst = line.at[:, :, d - zme * 8], x.at[own, :, yme]
            remote(src, dst, send1.at[1], recv1.at[1], d, dom).start()
        for k in range(unit):
            for z in range(planes):
                x[unit + k, z, yme] = line[k, z, yme]

    loads[2].wait()
    mass(1)
    mass(2)
    pl.when((me == gate) | (zme != gate // 8))(lambda: pl.semaphore_wait(hello.at[3], 7))
    pl.when((me != gate) & (zme == gate // 8))(lambda: pl.semaphore_wait(hello.at[3], 6))
    go(0)
    for e in range(6):
        @pl.when(me != home[e])
        def _():
            remote(we.at[e], xe.at[me], send_e.at[e], recv_e.at[6], home[e], dom).start()
    go(2)
    for t in range(3):
        stack(t)
    stiff(0)
    relay()
    stiff(1)
    stiff(2)
    loads[3].wait()
    loads[4].wait()

    def apply(value):
        high, low = halves(value)
        dot = functools.partial(jnp.dot, preferred_element_type=F32)
        return dot(chi[...], high) + (dot(clo[...], high) + dot(chi[...], low))

    def transform(n):
        a, size = spans[n]
        if n == 1:
            drain(recv1.at[1], w.at[own, pl.ds(0, 7 * planes)])
        else:
            arrived(recv1, w, n)
            for r in range(a, a + size):
                x[r, zme, yme] = w[r, me]
        for r in range(a, a + size, 2):
            two = range(r, min(r + 2, a + size))
            value = apply(jnp.concatenate([x[k].reshape(length, LANES) for k in two], axis=1))
            for m, k in enumerate(two):
                back[k] = value[:, LANES * m : LANES * m + LANES].reshape(count, depth, LANES)
        for r in range(a, a + size):
            q[r, me] = back[r, me]

    square = lax.broadcasted_iota(jnp.int32, (LANES, LANES), 0)
    hot = (jnp.broadcast_to(slot_ref[0:1, :], (LANES, LANES)) == square).astype(BF16)
    index = lane.astype(F32).astype(BF16)
    inverse = lax.dot_general(index, hot, (((1,), (1,)), ((), ())), preferred_element_type=F32).astype(jnp.int32)
    below, lower = lane < LANES - EY, lane % EY < 7
    lane8 = lane[0:8]

    def row(c, i, j):
        n = place(c, i, j)
        return v[c, 8 * i + j] + (q[n // count, n % count] if n < 192 else qe[n - 192])

    faces = [
        remote(to_left, from_right, send_f.at[0], recv_f.at[0], me, before),
        remote(to_right, from_left, send_f.at[1], recv_f.at[1], me, after),
    ]

    def pack(ref, values):
        last = jnp.zeros((8, LANES), F32)
        for c, value in enumerate(values):
            upper_planes, lower_planes = value[0:8], value[8:16]
            ref[c] = jnp.where(lane8 < 64, upper_planes, turn(lower_planes, 64))
            last = jnp.where(lane8 == 2 * c, turn(upper_planes, 64 + 2 * c), last)
            last = jnp.where(lane8 == 2 * c + 1, turn(lower_planes, 65 + 2 * c), last)
        ref[3] = last

    def unpack(ref, c):
        main, last = ref[c], ref[3]
        pick = lambda value, k: jnp.where(lane8 == 64, turn(last, 64 - 2 * c - k), value)
        return jnp.concatenate([pick(main, 0), pick(turn(main, 64), 1)], axis=0)

    def send_faces():
        lefts, rights = [], []
        for c in range(3):
            for k in range(2):
                n = 24 + 2 * c + k
                ve[2 * c + k] = ve[2 * c + k] + q[n // count, n % count]
            value = turn(ve[2 * c], 64)
            for j in range(8):
                value = jnp.where(lane // EY == j, turn(row(c, 0, j), EY * j), value)
            lefts.append(value)
            rights.append(ve[2 * c + 1])
        pack(to_left, lefts)
        pack(to_right, rights)
        for copy in faces:
            copy.start()

    def expand(c, parts):
        def put(n, value):
            out[c, n] = jnp.take_along_axis(value, inverse, axis=1)

        came = unpack(from_left, c)
        edge = ve[2 * c] + jnp.where(lane == 0, turn(came, 64), 0.0)
        if 0 in parts:
            face = ve[2 * c + 1] + unpack(from_right, c)
        for i in parts:
            for j in range(8):
                value = row(c, i, j)
                if i == 0:
                    value = value + jnp.where(lane < EY, turn(came, -EY * j), 0.0)
                    right = jnp.where(below, turn(value, -EY), turn(face, LANES - EY - EY * j))
                    put(72 + j, right)
                if j == 0:
                    top = jnp.where(lower, turn(value, -1), turn(edge, 7 - i))
                    put(9 * i + 8, top)
                    if i == 0:
                        corner = jnp.where(below, turn(top, -EY), turn(face, 63))
                        put(80, jnp.where(lower, turn(right, -1), corner))
                put(9 * i + j, value)

    @pl.when(me == gate)
    def _():
        for n, other in enumerate((before, after)):
            signal(hello.at[n], me, other)

    transform(0)
    come(0)
    go(3)
    go(4)

    @pl.when(me == gate)
    def _():
        for n in range(2):
            pl.semaphore_wait(hello.at[n], 1)
        peers(lambda d: signal(hello.at[2], d, dom))

    transform(1)
    transform(2)
    arrived(recv2, q, 0)
    pl.when(me != gate)(lambda: pl.semaphore_wait(hello.at[2], 1))
    send_faces()
    come(1)
    come(2)
    for e in range(6):
        @pl.when(me == home[e])
        def _():
            xe[me] = we[e]
            drain(recv_e.at[6], xe.at[rest])
            backe[...] = apply(xe[...].reshape(length, LANES)).reshape(count, depth, LANES)
            qe[e] = backe[me]
            peers(lambda s: remote(backe.at[s], qe.at[e], send_e.at[6], recv_e.at[e], s, dom).start())

    for n in (3, 4):
        transform(n)
        come(n)

    arrived(recv2, q, 1)
    arrived(recv2, q, 2)
    for copy in faces:
        copy.wait()
    expand(0, range(8))
    for e in range(6):
        pl.when(me != home[e])(lambda: drain(recv_e.at[e], qe.at[0]))
    arrived(recv2, q, 3)
    expand(1, range(8))
    expand(2, (0, 1, 2, 7))
    arrived(recv2, q, 4)
    expand(2, (3, 4, 5, 6))

    for n in range(5):
        if n == 1:
            drain(send1.at[1], w.at[own, pl.ds(0, 7 * planes)])
        else:
            arrived(send1, w, n)
        arrived(send2, w, n)
    if planes > 1:
        drain(send_z.at[0], line.at[:, pl.ds(0, planes - 1)])
    for e in range(6):
        pl.when(me != home[e])(lambda: drain(send_e.at[e], we.at[0]))
        pl.when(me == home[e])(lambda: drain(send_e.at[6], xe.at[rest]))


def step(slots, geometry, mats, chi, clo, velocity):
    count, doms = lax.axis_size("modes"), lax.axis_size("dom")
    depth = velocity.shape[1] // NODES
    wire = (6 * 32 // count, count, depth, LANES)
    ends = (6, depth, LANES)
    single = (count, depth, LANES)
    face = (4, depth // 2, LANES)
    vmem, dma = pltpu.VMEM, pltpu.SemaphoreType.DMA
    there = pl.BlockSpec(memory_space=pl.ANY)
    return pl.pallas_call(
        functools.partial(kernel, count, doms, depth),
        in_specs=[there] * 6,
        out_specs=pl.BlockSpec(memory_space=pltpu.VMEM),
        out_shape=pltpu.VMEM((3, NODES, depth, LANES), F32),
        scratch_shapes=[
            vmem(slots.shape, jnp.int32),
            vmem(geometry.shape, F32),
            vmem(mats.shape, F32),
            vmem((3, NODES * depth, LANES), F32),
            vmem(chi.shape, BF16),
            vmem(clo.shape, BF16),
            vmem((TALL, LANES), F32),
            vmem((4 * TALL, 2 * LANES), BF16),
            vmem((3 * depth // 2, 256, 2 * LANES), BF16),
            vmem((TALL * depth, LANES), F32),
            vmem(wire, F32),
            vmem(ends, F32),
            vmem((3, ROWS, depth, LANES), F32),
            vmem(ends, F32),
            vmem((wire[0] // 6, count // 8, 8) + wire[2:], F32),
            vmem((wire[0], count // 8, 8) + wire[2:], F32),
            vmem(single, F32),
            vmem(wire, F32),
            vmem(single, F32),
            vmem(wire, F32),
            vmem(ends, F32),
            vmem(face, F32),
            vmem(face, F32),
            vmem(face, F32),
            vmem(face, F32),
            dma((8,)),
            dma((1,)),
            dma((1,)),
            dma((5,)),
            dma((5,)),
            dma((5,)),
            dma((5,)),
            dma((7,)),
            dma((7,)),
            dma((2,)),
            dma((2,)),
            pltpu.SemaphoreType.REGULAR((4,)),
        ],
        compiler_params=pltpu.CompilerParams(collective_id=0, has_side_effects=True),
        name="step",
    )(slots, geometry, mats, chi, clo, velocity)


def body(velocity, slot_of_cell, elem_mats, geometry):
    depth = velocity.shape[1]
    table = coupling(depth * lax.axis_size("modes"))
    chi = np.asarray(table, np.float32).astype(jnp.bfloat16)
    clo = (table - chi.astype(np.float64)).astype(np.float32).astype(jnp.bfloat16)
    flat = jnp.swapaxes(velocity, 1, 2).reshape(3, NODES * depth, LANES)
    result = step(slot_of_cell, geometry, jnp.swapaxes(elem_mats, 0, 1), jnp.asarray(chi), jnp.asarray(clo), flat)
    return jnp.swapaxes(result, 1, 2)


def solution(mesh):
    in_specs = (P(None, "modes", None, "dom"), P("dom", None), P(), P(None, "dom"))
    out_specs = P(None, "modes", None, "dom")
    return jax.shard_map(body, mesh=mesh, in_specs=in_specs, out_specs=out_specs, check_vma=False)
```

```python
import functools

import jax
import jax.numpy as jnp
import numpy as np
from jax import lax
from jax.experimental import pallas as pl
from jax.experimental.pallas import tpu as pltpu
from jax.sharding import PartitionSpec as P

MESH = pl.DeviceIdType.MESH
F32, BF16 = jnp.float32, jnp.bfloat16
LANES = 128
EY = 8
ROWS = 64
NODES = 81
TALL = 88


def coupling(length):
    index = np.arange(length)
    half = length // 2
    wave = np.where(index <= half, index, index - half)
    angle = 2.0 * np.pi * ((wave[:, None] * index[None, :]) % length) / length
    table = np.where((index <= half)[:, None], np.cos(angle), np.sin(angle))
    weight = np.where((index == 0) | (index == half), 1.0, 2.0) / length
    scale = weight * (8.0 * wave / length) ** 2
    return (table.T * scale) @ table


def halves(x):
    high = x.astype(BF16)
    return high, (x - high.astype(F32)).astype(BF16)


def turn(value, shift):
    shift = shift % LANES
    return pltpu.roll(value, shift, 1) if shift else value


def homes(count):
    return [8, 19, 13, 22, 3, 28] if count == 32 else list(range(6))


def place(c, i, j):
    if i == 0:
        return 8 * c + j
    if c == 0:
        return 24 + 8 * i + j
    if c == 1:
        return 80 + 8 * i + j
    return (30 + j if j < 2 else 190 + j) if i == 7 else 136 + 8 * i + j


def kernel(
    count, doms, depth,
    slot_hbm, geo_hbm, mats_hbm, chi_hbm, clo_hbm, vel_hbm, out,
    slot_ref, geo_ref, mats_ref, vel, chi, clo, stage, lhs, rhs, tall,
    w, we, v, ve, line, x, xe, back, backe, q, qe, to_left, to_right, from_left, from_right,
    end_left, end_right, end_from_left, end_from_right,
    load, send_z, recv_z, send1, recv1, send2, recv2, send_e, recv_e, send_f, recv_f, hello,
):
    unit = 32 // count
    chunks = [(0, 1), (1, 2), (2, 3), (3, 5), (5, 6)]
    spans = [(unit * a, unit * (b - a)) for a, b in chunks]
    length = depth * count
    me, dom = lax.axis_index("modes"), lax.axis_index("dom")
    after, before = lax.rem(dom + 1, doms), lax.rem(dom + doms - 1, doms)
    home = homes(count)

    def remote(src, dst, send, recv, modes, where):
        return pltpu.make_async_remote_copy(
            src_ref=src, dst_ref=dst, send_sem=send, recv_sem=recv, device_id=(modes, where), device_id_type=MESH
        )

    def drain(sem, ref):
        pltpu.make_async_copy(ref, ref, sem).wait()

    planes = count // 8

    order = [2, 1, 3, 0] if planes == 4 else range(planes)

    def peers(act):
        for high in order:
            def some(n, _):
                z = lax.rem(me // 8 + high, planes)
                act(z * 8 + lax.rem(lax.rem(me, 8) + n, 8))
                return 0

            lax.fori_loop(2 if high else 1, 10 if high else 8, some, 0)

    loads = [pltpu.make_async_copy(vel_hbm.at[c], vel.at[c], load.at[c]) for c in range(3)]
    loads += [pltpu.make_async_copy(chi_hbm, chi, load.at[3]), pltpu.make_async_copy(clo_hbm, clo, load.at[4])]
    small = ((slot_hbm, slot_ref), (geo_hbm, geo_ref), (mats_hbm, mats_ref))
    loads += [pltpu.make_async_copy(src, dst, load.at[5 + n]) for n, (src, dst) in enumerate(small)]
    barrier = pltpu.get_barrier_semaphore()
    gate = max(count // 2 - 4, 0)
    zme, yme = me // 8, lax.rem(me, 8)
    line_peers = [lax.rem(zme + high, planes) * 8 + yme for high in range(1, planes)]
    plane_peers = [zme * 8 + lax.rem(yme + low, 8) for low in range(1, 8)]
    heard = planes - 1 + 7

    def signal(sem, modes, where):
        pl.semaphore_signal(sem, inc=1, device_id=(modes, where), device_id_type=MESH)

    for d in line_peers + plane_peers:
        signal(barrier, d, dom)

    @pl.when((yme == gate % 8) & (zme != gate // 8))
    def _():
        signal(barrier, gate + 1, dom)

    @pl.when(me == gate)
    def _():
        for other in (before, after):
            signal(barrier, me, other)

    for n in (7, 5, 6, 0, 1, 2, 3, 4):
        loads[n].start()
    for n in (5, 6, 7):
        loads[n].wait()

    wide = lax.broadcasted_iota(jnp.int32, (TALL, LANES), 1)

    def stack(t):
        stage[...] = jnp.zeros_like(stage)
        for i in range(8):
            stage[8 * i : 8 * i + 8, 0:NODES] = mats_ref[9 * i : 9 * i + 8, t, :]
            stage[72 + i : 73 + i, 0:NODES] = mats_ref[9 * i + 8 : 9 * i + 9, t, :]
        stage[64:72, 0:NODES] = mats_ref[72:80, t, :]
        stage[80:81, 0:NODES] = mats_ref[80:81, t, :]
        full = stage[...]
        high = full.astype(BF16).astype(F32)
        low = full - high
        low_turned = turn(low, 80)
        first = jnp.where(wide < 80, high, low_turned)
        second = jnp.where(wide < 32, low_turned, turn(high, 32))
        second = jnp.where(wide == 113, turn(low, 33), jnp.where(wide == 114, turn(high, 34), second))
        second = jnp.where(wide < 115, second, 0.0)
        lhs[TALL * t : TALL * t + TALL, 0:LANES] = first.astype(BF16)
        lhs[TALL * t : TALL * t + TALL, LANES:] = second.astype(BF16)

    stack(3)
    slots = jnp.broadcast_to(slot_ref[0:1, :], (80, LANES))
    geo = [
        jnp.take_along_axis(jnp.broadcast_to(geo_ref[t : t + 1, :], (8, LANES)), slots[0:8], axis=1)[0:1] for t in range(4)
    ]
    row16 = lax.broadcasted_iota(jnp.int32, (16, LANES), 0)
    lane = lax.broadcasted_iota(jnp.int32, (depth, LANES), 1)
    inner, upper = lane >= EY, lane % EY >= 1

    def columns(c, p):
        def product(lo, size):
            part = lambda m: vel[m, pl.ds(lo * depth + p, size, stride=depth), :]
            return jnp.take_along_axis(part(c) * part((c + 1) % 3), slots[0:size], axis=1)

        high, low = halves(product(0, 80))
        last = product(73, 8)[7:8]
        last_high = last.astype(BF16).astype(F32)
        rest = jnp.where(row16 < 2, last_high, jnp.where(row16 == 2, last - last_high, 0.0))
        return jnp.concatenate([high, high, low, rest.astype(BF16)], axis=0)

    def assemble(rows, ends):
        at = lambda r: tall[r * depth : r * depth + depth, :]
        corner = at(80)
        edge = jnp.zeros((depth, LANES), F32)
        face = jnp.where(lane == 64, turn(corner, 65), 0.0)
        for i in range(8):
            top = at(72 + i)
            if i == 0:
                top = top + jnp.where(inner, turn(corner, EY), 0.0)
            edge = jnp.where(lane % EY == i, turn(top, i - 7), edge)
            for j in range(8):
                value = at(8 * i + j)
                if i == 0:
                    value = value + jnp.where(inner, turn(at(64 + j), EY), 0.0)
                if j == 0:
                    value = value + jnp.where(upper, turn(top, 1), 0.0)
                rows(i, j, value)
        for j in range(8):
            right = at(64 + j)
            if j == 0:
                right = right + jnp.where(upper, turn(corner, 1), 0.0)
            face = jnp.where(lane // EY == j, turn(right, EY + EY * j), face)
        ends(edge, face)

    def mass(c):
        scale = jnp.broadcast_to(geo[3], (TALL, LANES))

        def pair(step, _):
            block = jnp.concatenate([columns(c, 2 * step), columns(c, 2 * step + 1)], axis=1)
            rhs[c * (depth // 2) + step] = block
            image = jnp.dot(lhs[3 * TALL :, :], block, preferred_element_type=F32)
            for h in range(2):
                tall[pl.ds(2 * step + h, TALL, stride=depth), :] = image[:, LANES * h : LANES * h + LANES] * scale
            return 0

        lax.fori_loop(0, depth // 2, pair, 0, unroll=2)

        def rows(i, j, value):
            n = place(c, i, j)
            if n < 192:
                w[n // count, n % count] = value
            else:
                we[n - 192] = value

        def ends(edge, face):
            for k, value in enumerate((edge, face)):
                w[(24 + 2 * c + k) // count, (24 + 2 * c + k) % count] = value

        assemble(rows, ends)

    def stiff(c):
        scale = [jnp.broadcast_to(g, (TALL, LANES)) for g in geo]

        def pair(step, _):
            image = jnp.dot(lhs[...], rhs[c * (depth // 2) + step], preferred_element_type=F32)
            for h in range(2):
                part = image[:, LANES * h : LANES * h + LANES]
                terms = [part[TALL * t : TALL * t + TALL] * scale[t] for t in range(4)]
                tall[pl.ds(2 * step + h, TALL, stride=depth), :] = (terms[0] + terms[1]) + (terms[2] + terms[3])
            return 0

        lax.fori_loop(0, depth // 2, pair, 0, unroll=2)

        def rows(i, j, value):
            v[c, 8 * i + j] = value

        def ends(edge, face):
            ve[2 * c], ve[2 * c + 1] = edge, face

        assemble(rows, ends)

    def go(n):
        a, size = spans[n]
        peers(lambda d: remote(w.at[pl.ds(a, size), d], x.at[pl.ds(a, size), zme, yme], send1.at[n], recv1.at[n], d, dom).start())

    def come(n):
        a, size = spans[n]
        peers(lambda s: remote(back.at[pl.ds(a, size), s], q.at[pl.ds(a, size), me], send2.at[n], recv2.at[n], s, dom).start())

    rest = pl.ds(0, count - 1)

    def arrived(sem, ref, n):
        drain(sem.at[n], ref.at[pl.ds(*spans[n]), rest])

    loads[0].wait()
    loads[1].wait()
    mass(0)
    pl.when((me != gate) & (me != gate + 1))(lambda: pl.semaphore_wait(barrier, heard))
    pl.when(me == gate)(lambda: pl.semaphore_wait(barrier, heard + 2))
    pl.when(me == gate + 1)(lambda: pl.semaphore_wait(barrier, heard + planes - 1))

    @pl.when(me != gate)
    def _():
        for d in plane_peers:
            signal(hello.at[3], d, dom)

    own = pl.ds(unit, unit)
    for d in line_peers:
        block = w.at[own, pl.ds(d - yme, 8)]
        remote(block, line.at[:, zme], send_z.at[0], recv_z.at[0], d, dom).start()
    for k in range(unit):
        for n in range(8):
            line[k, zme, n] = w[unit + k, zme * 8 + n]

    def relay():
        if planes > 1:
            drain(recv_z.at[0], line.at[:, pl.ds(0, planes - 1)])
        for d in plane_peers:
            src, dst = line.at[:, :, d - zme * 8], x.at[own, :, yme]
            remote(src, dst, send1.at[1], recv1.at[1], d, dom).start()
        for k in range(unit):
            for z in range(planes):
                x[unit + k, z, yme] = line[k, z, yme]

    loads[2].wait()
    mass(1)
    mass(2)
    pl.when((me == gate) | (zme != gate // 8))(lambda: pl.semaphore_wait(hello.at[3], 7))
    pl.when((me != gate) & (zme == gate // 8))(lambda: pl.semaphore_wait(hello.at[3], 6))
    go(0)
    for e in range(6):
        @pl.when(me != home[e])
        def _():
            remote(we.at[e], xe.at[me], send_e.at[e], recv_e.at[6], home[e], dom).start()
    go(2)
    for t in range(3):
        stack(t)
    stiff(0)
    relay()
    stiff(1)
    stiff(2)
    loads[3].wait()
    loads[4].wait()

    def apply(value):
        high, low = halves(value)
        dot = functools.partial(jnp.dot, preferred_element_type=F32)
        return dot(chi[...], high) + (dot(clo[...], high) + dot(chi[...], low))

    def transform(n):
        a, size = spans[n]
        if n == 1:
            drain(recv1.at[1], w.at[own, pl.ds(0, 7 * planes)])
        else:
            arrived(recv1, w, n)
            for r in range(a, a + size):
                x[r, zme, yme] = w[r, me]
        for r in range(a, a + size, 2):
            two = range(r, min(r + 2, a + size))
            value = apply(jnp.concatenate([x[k].reshape(length, LANES) for k in two], axis=1))
            for m, k in enumerate(two):
                back[k] = value[:, LANES * m : LANES * m + LANES].reshape(count, depth, LANES)
        for r in range(a, a + size):
            q[r, me] = back[r, me]

    square = lax.broadcasted_iota(jnp.int32, (LANES, LANES), 0)
    hot = (jnp.broadcast_to(slot_ref[0:1, :], (LANES, LANES)) == square).astype(BF16)
    index = lane.astype(F32).astype(BF16)
    inverse = lax.dot_general(index, hot, (((1,), (1,)), ((), ())), preferred_element_type=F32).astype(jnp.int32)
    below, lower = lane < LANES - EY, lane % EY < 7
    lane8 = lane[0:8]

    def row(c, i, j):
        n = place(c, i, j)
        return v[c, 8 * i + j] + (q[n // count, n % count] if n < 192 else qe[n - 192])

    faces = [
        remote(to_left, from_right, send_f.at[0], recv_f.at[0], me, before),
        remote(to_right, from_left, send_f.at[1], recv_f.at[1], me, after),
        remote(end_left, end_from_right, send_f.at[2], recv_f.at[2], me, before),
        remote(end_right, end_from_left, send_f.at[3], recv_f.at[3], me, after),
    ]

    plane = lax.broadcasted_iota(jnp.int32, (depth, LANES), 0)

    def pack(ref, end, values):
        last = jnp.zeros((depth, LANES), F32)
        for c, value in enumerate(values):
            ref[c] = jnp.where(lane8 < 64, value[0:8], turn(value[8:16], 64))
            last = jnp.where(lane == depth * c + plane, jnp.broadcast_to(value[:, 64:65], (depth, LANES)), last)
        end[...] = jnp.sum(last, axis=0, keepdims=True)

    def unpack(ref, end, c):
        last = jnp.where(lane == depth * c + plane, jnp.broadcast_to(end[...], (depth, LANES)), 0.0)
        value = jnp.concatenate([ref[c], turn(ref[c], 64)], axis=0)
        return jnp.where(lane == 64, jnp.sum(last, axis=1, keepdims=True), value)

    def send_faces():
        lefts, rights = [], []
        for c in range(3):
            for k in range(2):
                n = 24 + 2 * c + k
                ve[2 * c + k] = ve[2 * c + k] + q[n // count, n % count]
            value = turn(ve[2 * c], 64)
            for j in range(8):
                value = jnp.where(lane // EY == j, turn(row(c, 0, j), EY * j), value)
            lefts.append(value)
            rights.append(ve[2 * c + 1])
        pack(to_left, end_left, lefts)
        pack(to_right, end_right, rights)
        for copy in faces:
            copy.start()

    def expand(c, parts):
        def put(n, value):
            out[c, n] = jnp.take_along_axis(value, inverse, axis=1)

        came = unpack(from_left, end_from_left, c)
        edge = ve[2 * c] + jnp.where(lane == 0, turn(came, 64), 0.0)
        if 0 in parts:
            face = ve[2 * c + 1] + unpack(from_right, end_from_right, c)
        for i in parts:
            for j in range(8):
                value = row(c, i, j)
                if i == 0:
                    value = value + jnp.where(lane < EY, turn(came, -EY * j), 0.0)
                    right = jnp.where(below, turn(value, -EY), turn(face, LANES - EY - EY * j))
                    put(72 + j, right)
                if j == 0:
                    top = jnp.where(lower, turn(value, -1), turn(edge, 7 - i))
                    put(9 * i + 8, top)
                    if i == 0:
                        corner = jnp.where(below, turn(top, -EY), turn(face, 63))
                        put(80, jnp.where(lower, turn(right, -1), corner))
                put(9 * i + j, value)

    @pl.when(me == gate)
    def _():
        for n, other in enumerate((before, after)):
            signal(hello.at[n], me, other)

    transform(0)
    come(0)
    go(3)
    go(4)

    @pl.when(me == gate)
    def _():
        for n in range(2):
            pl.semaphore_wait(hello.at[n], 1)
        peers(lambda d: signal(hello.at[2], d, dom))

    transform(1)
    transform(2)
    arrived(recv2, q, 0)
    pl.when(me != gate)(lambda: pl.semaphore_wait(hello.at[2], 1))
    send_faces()
    come(1)
    come(2)
    for e in range(6):
        @pl.when(me == home[e])
        def _():
            xe[me] = we[e]
            drain(recv_e.at[6], xe.at[rest])
            backe[...] = apply(xe[...].reshape(length, LANES)).reshape(count, depth, LANES)
            qe[e] = backe[me]
            peers(lambda s: remote(backe.at[s], qe.at[e], send_e.at[6], recv_e.at[e], s, dom).start())

    for n in (3, 4):
        transform(n)
        come(n)

    arrived(recv2, q, 1)
    arrived(recv2, q, 2)
    for copy in faces:
        copy.wait()
    expand(0, range(8))
    for e in range(6):
        pl.when(me != home[e])(lambda: drain(recv_e.at[e], qe.at[0]))
    arrived(recv2, q, 3)
    expand(1, range(8))
    expand(2, (0, 1, 2, 7))
    arrived(recv2, q, 4)
    expand(2, (3, 4, 5, 6))

    for n in range(5):
        if n == 1:
            drain(send1.at[1], w.at[own, pl.ds(0, 7 * planes)])
        else:
            arrived(send1, w, n)
        arrived(send2, w, n)
    if planes > 1:
        drain(send_z.at[0], line.at[:, pl.ds(0, planes - 1)])
    for e in range(6):
        pl.when(me != home[e])(lambda: drain(send_e.at[e], we.at[0]))
        pl.when(me == home[e])(lambda: drain(send_e.at[6], xe.at[rest]))


def step(slots, geometry, mats, chi, clo, velocity):
    count, doms = lax.axis_size("modes"), lax.axis_size("dom")
    depth = velocity.shape[1] // NODES
    wire = (6 * 32 // count, count, depth, LANES)
    ends = (6, depth, LANES)
    single = (count, depth, LANES)
    face, end = (3, depth // 2, LANES), (1, LANES)
    vmem, dma = pltpu.VMEM, pltpu.SemaphoreType.DMA
    there = pl.BlockSpec(memory_space=pl.ANY)
    return pl.pallas_call(
        functools.partial(kernel, count, doms, depth),
        in_specs=[there] * 6,
        out_specs=pl.BlockSpec(memory_space=pltpu.VMEM),
        out_shape=pltpu.VMEM((3, NODES, depth, LANES), F32),
        scratch_shapes=[
            vmem(slots.shape, jnp.int32),
            vmem(geometry.shape, F32),
            vmem(mats.shape, F32),
            vmem((3, NODES * depth, LANES), F32),
            vmem(chi.shape, BF16),
            vmem(clo.shape, BF16),
            vmem((TALL, LANES), F32),
            vmem((4 * TALL, 2 * LANES), BF16),
            vmem((3 * depth // 2, 256, 2 * LANES), BF16),
            vmem((TALL * depth, LANES), F32),
            vmem(wire, F32),
            vmem(ends, F32),
            vmem((3, ROWS, depth, LANES), F32),
            vmem(ends, F32),
            vmem((wire[0] // 6, count // 8, 8) + wire[2:], F32),
            vmem((wire[0], count // 8, 8) + wire[2:], F32),
            vmem(single, F32),
            vmem(wire, F32),
            vmem(single, F32),
            vmem(wire, F32),
            vmem(ends, F32),
            vmem(face, F32),
            vmem(face, F32),
            vmem(face, F32),
            vmem(face, F32),
            vmem(end, F32),
            vmem(end, F32),
            vmem(end, F32),
            vmem(end, F32),
            dma((8,)),
            dma((1,)),
            dma((1,)),
            dma((5,)),
            dma((5,)),
            dma((5,)),
            dma((5,)),
            dma((7,)),
            dma((7,)),
            dma((4,)),
            dma((4,)),
            pltpu.SemaphoreType.REGULAR((4,)),
        ],
        compiler_params=pltpu.CompilerParams(collective_id=0, has_side_effects=True),
        name="step",
    )(slots, geometry, mats, chi, clo, velocity)


def body(velocity, slot_of_cell, elem_mats, geometry):
    depth = velocity.shape[1]
    table = coupling(depth * lax.axis_size("modes"))
    chi = np.asarray(table, np.float32).astype(jnp.bfloat16)
    clo = (table - chi.astype(np.float64)).astype(np.float32).astype(jnp.bfloat16)
    flat = jnp.swapaxes(velocity, 1, 2).reshape(3, NODES * depth, LANES)
    result = step(slot_of_cell, geometry, jnp.swapaxes(elem_mats, 0, 1), jnp.asarray(chi), jnp.asarray(clo), flat)
    return jnp.swapaxes(result, 1, 2)


def solution(mesh):
    in_specs = (P(None, "modes", None, "dom"), P("dom", None), P(), P(None, "dom"))
    out_specs = P(None, "modes", None, "dom")
    return jax.shard_map(body, mesh=mesh, in_specs=in_specs, out_specs=out_specs, check_vma=False)
```

```python
import functools

import jax
import jax.numpy as jnp
import numpy as np
from jax import lax
from jax.experimental import pallas as pl
from jax.experimental.pallas import tpu as pltpu
from jax.sharding import PartitionSpec as P

MESH = pl.DeviceIdType.MESH
F32, BF16 = jnp.float32, jnp.bfloat16
LANES = 128
EY = 8
ROWS = 64
NODES = 81
TALL = 88


def coupling(length):
    index = np.arange(length)
    half = length // 2
    wave = np.where(index <= half, index, index - half)
    angle = 2.0 * np.pi * ((wave[:, None] * index[None, :]) % length) / length
    table = np.where((index <= half)[:, None], np.cos(angle), np.sin(angle))
    weight = np.where((index == 0) | (index == half), 1.0, 2.0) / length
    scale = weight * (8.0 * wave / length) ** 2
    return (table.T * scale) @ table


def halves(x):
    high = x.astype(BF16)
    return high, (x - high.astype(F32)).astype(BF16)


def turn(value, shift):
    shift = shift % LANES
    return pltpu.roll(value, shift, 1) if shift else value


def homes(count):
    return [0, 27, 5, 30, 2, 29] if count == 32 else list(range(6))


def place(c, i, j):
    if i == 0:
        return 8 * c + j
    if c == 0:
        return 24 + 8 * i + j
    if c == 1:
        return 80 + 8 * i + j
    return (30 + j if j < 2 else 190 + j) if i == 7 else 136 + 8 * i + j


def kernel(
    count, doms, depth,
    slot_hbm, geo_hbm, mats_hbm, chi_hbm, clo_hbm, vel_hbm, out,
    slot_ref, geo_ref, mats_ref, vel, chi, clo, stage, lhs, rhs, tall,
    w, we, v, ve, line, x, xe, back, backe, q, qe, to_left, to_right, from_left, from_right,
    end_left, end_right, end_from_left, end_from_right,
    load, send_z, recv_z, send1, recv1, send2, recv2, send_e, recv_e, send_f, recv_f, hello,
):
    unit = 32 // count
    chunks = [(0, 1), (1, 2), (2, 3), (3, 5), (5, 6)]
    spans = [(unit * a, unit * (b - a)) for a, b in chunks]
    length = depth * count
    me, dom = lax.axis_index("modes"), lax.axis_index("dom")
    after, before = lax.rem(dom + 1, doms), lax.rem(dom + doms - 1, doms)
    home = homes(count)

    def remote(src, dst, send, recv, modes, where):
        return pltpu.make_async_remote_copy(
            src_ref=src, dst_ref=dst, send_sem=send, recv_sem=recv, device_id=(modes, where), device_id_type=MESH
        )

    def drain(sem, ref):
        pltpu.make_async_copy(ref, ref, sem).wait()

    planes = count // 8

    order = [2, 3, 1, 0] if planes == 4 else range(planes)

    def peers(act):
        for high in order:
            def some(n, _):
                z = lax.rem(me // 8 + high, planes)
                act(z * 8 + lax.rem(lax.rem(me, 8) + n, 8))
                return 0

            lax.fori_loop(2 if high else 1, 10 if high else 8, some, 0)

    loads = [pltpu.make_async_copy(vel_hbm.at[c], vel.at[c], load.at[c]) for c in range(3)]
    loads += [pltpu.make_async_copy(chi_hbm, chi, load.at[3]), pltpu.make_async_copy(clo_hbm, clo, load.at[4])]
    small = ((slot_hbm, slot_ref), (geo_hbm, geo_ref), (mats_hbm, mats_ref))
    loads += [pltpu.make_async_copy(src, dst, load.at[5 + n]) for n, (src, dst) in enumerate(small)]
    barrier = pltpu.get_barrier_semaphore()
    gate = max(count // 2 - 4, 0)
    zme, yme = me // 8, lax.rem(me, 8)
    line_peers = [lax.rem(zme + high, planes) * 8 + yme for high in range(1, planes)]
    plane_peers = [zme * 8 + lax.rem(yme + low, 8) for low in range(1, 8)]
    heard = planes - 1 + 7

    def signal(sem, modes, where):
        pl.semaphore_signal(sem, inc=1, device_id=(modes, where), device_id_type=MESH)

    for d in line_peers + plane_peers:
        signal(barrier, d, dom)

    @pl.when((yme == gate % 8) & (zme != gate // 8))
    def _():
        signal(barrier, gate + 1, dom)

    @pl.when(me == gate)
    def _():
        for other in (before, after):
            signal(barrier, me, other)

    for n in (7, 5, 6, 0, 1, 2, 3, 4):
        loads[n].start()
    for n in (5, 6, 7):
        loads[n].wait()

    wide = lax.broadcasted_iota(jnp.int32, (TALL, LANES), 1)

    def stack(t):
        stage[...] = jnp.zeros_like(stage)
        for i in range(8):
            stage[8 * i : 8 * i + 8, 0:NODES] = mats_ref[9 * i : 9 * i + 8, t, :]
            stage[72 + i : 73 + i, 0:NODES] = mats_ref[9 * i + 8 : 9 * i + 9, t, :]
        stage[64:72, 0:NODES] = mats_ref[72:80, t, :]
        stage[80:81, 0:NODES] = mats_ref[80:81, t, :]
        full = stage[...]
        high = full.astype(BF16).astype(F32)
        low = full - high
        low_turned = turn(low, 80)
        first = jnp.where(wide < 80, high, low_turned)
        second = jnp.where(wide < 32, low_turned, turn(high, 32))
        second = jnp.where(wide == 113, turn(low, 33), jnp.where(wide == 114, turn(high, 34), second))
        second = jnp.where(wide < 115, second, 0.0)
        lhs[TALL * t : TALL * t + TALL, 0:LANES] = first.astype(BF16)
        lhs[TALL * t : TALL * t + TALL, LANES:] = second.astype(BF16)

    stack(3)
    slots = jnp.broadcast_to(slot_ref[0:1, :], (80, LANES))
    geo = [
        jnp.take_along_axis(jnp.broadcast_to(geo_ref[t : t + 1, :], (8, LANES)), slots[0:8], axis=1)[0:1] for t in range(4)
    ]
    row16 = lax.broadcasted_iota(jnp.int32, (16, LANES), 0)
    lane = lax.broadcasted_iota(jnp.int32, (depth, LANES), 1)
    inner, upper = lane >= EY, lane % EY >= 1

    def columns(c, p):
        def product(lo, size):
            part = lambda m: vel[m, pl.ds(lo * depth + p, size, stride=depth), :]
            return jnp.take_along_axis(part(c) * part((c + 1) % 3), slots[0:size], axis=1)

        high, low = halves(product(0, 80))
        last = product(73, 8)[7:8]
        last_high = last.astype(BF16).astype(F32)
        rest = jnp.where(row16 < 2, last_high, jnp.where(row16 == 2, last - last_high, 0.0))
        return jnp.concatenate([high, high, low, rest.astype(BF16)], axis=0)

    def assemble(rows, ends):
        at = lambda r: tall[r * depth : r * depth + depth, :]
        corner = at(80)
        edge = jnp.zeros((depth, LANES), F32)
        face = jnp.where(lane == 64, turn(corner, 65), 0.0)
        for i in range(8):
            top = at(72 + i)
            if i == 0:
                top = top + jnp.where(inner, turn(corner, EY), 0.0)
            edge = jnp.where(lane % EY == i, turn(top, i - 7), edge)
            for j in range(8):
                value = at(8 * i + j)
                if i == 0:
                    value = value + jnp.where(inner, turn(at(64 + j), EY), 0.0)
                if j == 0:
                    value = value + jnp.where(upper, turn(top, 1), 0.0)
                rows(i, j, value)
        for j in range(8):
            right = at(64 + j)
            if j == 0:
                right = right + jnp.where(upper, turn(corner, 1), 0.0)
            face = jnp.where(lane // EY == j, turn(right, EY + EY * j), face)
        ends(edge, face)

    def mass(c):
        scale = jnp.broadcast_to(geo[3], (TALL, LANES))

        def pair(step, _):
            block = jnp.concatenate([columns(c, 2 * step), columns(c, 2 * step + 1)], axis=1)
            rhs[c * (depth // 2) + step] = block
            image = jnp.dot(lhs[3 * TALL :, :], block, preferred_element_type=F32)
            for h in range(2):
                tall[pl.ds(2 * step + h, TALL, stride=depth), :] = image[:, LANES * h : LANES * h + LANES] * scale
            return 0

        lax.fori_loop(0, depth // 2, pair, 0, unroll=4)

        def rows(i, j, value):
            n = place(c, i, j)
            if n < 192:
                w[n // count, n % count] = value
            else:
                we[n - 192] = value

        def ends(edge, face):
            for k, value in enumerate((edge, face)):
                w[(24 + 2 * c + k) // count, (24 + 2 * c + k) % count] = value

        assemble(rows, ends)

    def stiff(c):
        scale = [jnp.broadcast_to(g, (TALL, LANES)) for g in geo]

        def pair(step, _):
            image = jnp.dot(lhs[...], rhs[c * (depth // 2) + step], preferred_element_type=F32)
            for h in range(2):
                part = image[:, LANES * h : LANES * h + LANES]
                terms = [part[TALL * t : TALL * t + TALL] * scale[t] for t in range(4)]
                tall[pl.ds(2 * step + h, TALL, stride=depth), :] = (terms[0] + terms[1]) + (terms[2] + terms[3])
            return 0

        lax.fori_loop(0, depth // 2, pair, 0, unroll=4)

        def rows(i, j, value):
            v[c, 8 * i + j] = value

        def ends(edge, face):
            ve[2 * c], ve[2 * c + 1] = edge, face

        assemble(rows, ends)

    def go(n):
        a, size = spans[n]
        peers(lambda d: remote(w.at[pl.ds(a, size), d], x.at[pl.ds(a, size), zme, yme], send1.at[n], recv1.at[n], d, dom).start())

    def come(n):
        a, size = spans[n]
        peers(lambda s: remote(back.at[pl.ds(a, size), s], q.at[pl.ds(a, size), me], send2.at[n], recv2.at[n], s, dom).start())

    rest = pl.ds(0, count - 1)

    def arrived(sem, ref, n):
        drain(sem.at[n], ref.at[pl.ds(*spans[n]), rest])

    loads[0].wait()
    loads[1].wait()
    mass(0)
    pl.when((me != gate) & (me != gate + 1))(lambda: pl.semaphore_wait(barrier, heard))
    pl.when(me == gate)(lambda: pl.semaphore_wait(barrier, heard + 2))
    pl.when(me == gate + 1)(lambda: pl.semaphore_wait(barrier, heard + planes - 1))

    @pl.when(me != gate)
    def _():
        for d in plane_peers:
            signal(hello.at[3], d, dom)

    own = pl.ds(unit, unit)
    for d in line_peers:
        block = w.at[own, pl.ds(d - yme, 8)]
        remote(block, line.at[:, zme], send_z.at[0], recv_z.at[0], d, dom).start()
    for k in range(unit):
        for n in range(8):
            line[k, zme, n] = w[unit + k, zme * 8 + n]

    def relay():
        if planes > 1:
            drain(recv_z.at[0], line.at[:, pl.ds(0, planes - 1)])
        for d in plane_peers:
            src, dst = line.at[:, :, d - zme * 8], x.at[own, :, yme]
            remote(src, dst, send1.at[1], recv1.at[1], d, dom).start()
        for k in range(unit):
            for z in range(planes):
                x[unit + k, z, yme] = line[k, z, yme]

    loads[2].wait()
    mass(1)
    mass(2)
    pl.when((me == gate) | (zme != gate // 8))(lambda: pl.semaphore_wait(hello.at[3], 7))
    pl.when((me != gate) & (zme == gate // 8))(lambda: pl.semaphore_wait(hello.at[3], 6))
    go(0)
    for e in range(6):
        @pl.when(me != home[e])
        def _():
            remote(we.at[e], xe.at[me], send_e.at[e], recv_e.at[6], home[e], dom).start()
    go(2)
    for t in range(3):
        stack(t)
    stiff(0)
    relay()
    stiff(1)
    stiff(2)
    loads[3].wait()
    loads[4].wait()

    def apply(value):
        high, low = halves(value)
        dot = functools.partial(jnp.dot, preferred_element_type=F32)
        return dot(chi[...], high) + (dot(clo[...], high) + dot(chi[...], low))

    def transform(n):
        a, size = spans[n]
        if n == 1:
            drain(recv1.at[1], w.at[own, pl.ds(0, 7 * planes)])
        else:
            arrived(recv1, w, n)
            for r in range(a, a + size):
                x[r, zme, yme] = w[r, me]
        for r in range(a, a + size, 2):
            two = range(r, min(r + 2, a + size))
            value = apply(jnp.concatenate([x[k].reshape(length, LANES) for k in two], axis=1))
            for m, k in enumerate(two):
                back[k] = value[:, LANES * m : LANES * m + LANES].reshape(count, depth, LANES)
        for r in range(a, a + size):
            q[r, me] = back[r, me]

    square = lax.broadcasted_iota(jnp.int32, (LANES, LANES), 0)
    hot = (jnp.broadcast_to(slot_ref[0:1, :], (LANES, LANES)) == square).astype(BF16)
    index = lane.astype(F32).astype(BF16)
    inverse = lax.dot_general(index, hot, (((1,), (1,)), ((), ())), preferred_element_type=F32).astype(jnp.int32)
    below, lower = lane < LANES - EY, lane % EY < 7
    lane8 = lane[0:8]

    def row(c, i, j):
        n = place(c, i, j)
        return v[c, 8 * i + j] + (q[n // count, n % count] if n < 192 else qe[n - 192])

    faces = [
        remote(to_left, from_right, send_f.at[0], recv_f.at[0], me, before),
        remote(to_right, from_left, send_f.at[1], recv_f.at[1], me, after),
        remote(end_left, end_from_right, send_f.at[2], recv_f.at[2], me, before),
        remote(end_right, end_from_left, send_f.at[3], recv_f.at[3], me, after),
    ]

    plane = lax.broadcasted_iota(jnp.int32, (depth, LANES), 0)

    def pack(ref, end, values):
        last = jnp.zeros((depth, LANES), F32)
        for c, value in enumerate(values):
            ref[c] = jnp.where(lane8 < 64, value[0:8], turn(value[8:16], 64))
            last = jnp.where(lane == depth * c + plane, jnp.broadcast_to(value[:, 64:65], (depth, LANES)), last)
        end[...] = jnp.sum(last, axis=0, keepdims=True)

    def unpack(ref, end, c):
        last = jnp.where(lane == depth * c + plane, jnp.broadcast_to(end[...], (depth, LANES)), 0.0)
        value = jnp.concatenate([ref[c], turn(ref[c], 64)], axis=0)
        return jnp.where(lane == 64, jnp.sum(last, axis=1, keepdims=True), value)

    def send_faces():
        lefts, rights = [], []
        for c in range(3):
            for k in range(2):
                n = 24 + 2 * c + k
                ve[2 * c + k] = ve[2 * c + k] + q[n // count, n % count]
            value = turn(ve[2 * c], 64)
            for j in range(8):
                value = jnp.where(lane // EY == j, turn(row(c, 0, j), EY * j), value)
            lefts.append(value)
            rights.append(ve[2 * c + 1])
        pack(to_left, end_left, lefts)
        pack(to_right, end_right, rights)
        for copy in faces:
            copy.start()

    def expand(c, parts):
        def put(n, value):
            out[c, n] = jnp.take_along_axis(value, inverse, axis=1)

        came = unpack(from_left, end_from_left, c)
        edge = ve[2 * c] + jnp.where(lane == 0, turn(came, 64), 0.0)
        if 0 in parts:
            face = ve[2 * c + 1] + unpack(from_right, end_from_right, c)
        for i in parts:
            for j in range(8):
                value = row(c, i, j)
                if i == 0:
                    value = value + jnp.where(lane < EY, turn(came, -EY * j), 0.0)
                    right = jnp.where(below, turn(value, -EY), turn(face, LANES - EY - EY * j))
                    put(72 + j, right)
                if j == 0:
                    top = jnp.where(lower, turn(value, -1), turn(edge, 7 - i))
                    put(9 * i + 8, top)
                    if i == 0:
                        corner = jnp.where(below, turn(top, -EY), turn(face, 63))
                        put(80, jnp.where(lower, turn(right, -1), corner))
                put(9 * i + j, value)

    @pl.when(me == gate)
    def _():
        for n, other in enumerate((before, after)):
            signal(hello.at[n], me, other)

    transform(0)
    come(0)
    go(3)
    go(4)

    @pl.when(me == gate)
    def _():
        for n in range(2):
            pl.semaphore_wait(hello.at[n], 1)
        peers(lambda d: signal(hello.at[2], d, dom))

    transform(1)
    transform(2)
    arrived(recv2, q, 0)
    pl.when(me != gate)(lambda: pl.semaphore_wait(hello.at[2], 1))
    send_faces()
    come(1)
    come(2)
    for e in range(6):
        @pl.when(me == home[e])
        def _():
            xe[me] = we[e]
            drain(recv_e.at[6], xe.at[rest])
            backe[...] = apply(xe[...].reshape(length, LANES)).reshape(count, depth, LANES)
            qe[e] = backe[me]
            peers(lambda s: remote(backe.at[s], qe.at[e], send_e.at[6], recv_e.at[e], s, dom).start())

    for n in (3, 4):
        transform(n)
        come(n)

    arrived(recv2, q, 1)
    arrived(recv2, q, 2)
    for copy in faces:
        copy.wait()
    expand(0, range(8))
    for e in range(6):
        pl.when(me != home[e])(lambda: drain(recv_e.at[e], qe.at[0]))
    arrived(recv2, q, 3)
    expand(1, range(8))
    expand(2, (0, 1, 2, 7))
    arrived(recv2, q, 4)
    expand(2, (3, 4, 5, 6))

    for n in range(5):
        if n == 1:
            drain(send1.at[1], w.at[own, pl.ds(0, 7 * planes)])
        else:
            arrived(send1, w, n)
        arrived(send2, w, n)
    if planes > 1:
        drain(send_z.at[0], line.at[:, pl.ds(0, planes - 1)])
    for e in range(6):
        pl.when(me != home[e])(lambda: drain(send_e.at[e], we.at[0]))
        pl.when(me == home[e])(lambda: drain(send_e.at[6], xe.at[rest]))


def step(slots, geometry, mats, chi, clo, velocity):
    count, doms = lax.axis_size("modes"), lax.axis_size("dom")
    depth = velocity.shape[1] // NODES
    wire = (6 * 32 // count, count, depth, LANES)
    ends = (6, depth, LANES)
    single = (count, depth, LANES)
    face, end = (3, depth // 2, LANES), (1, LANES)
    vmem, dma = pltpu.VMEM, pltpu.SemaphoreType.DMA
    there = pl.BlockSpec(memory_space=pl.ANY)
    return pl.pallas_call(
        functools.partial(kernel, count, doms, depth),
        in_specs=[there] * 6,
        out_specs=pl.BlockSpec(memory_space=pltpu.VMEM),
        out_shape=pltpu.VMEM((3, NODES, depth, LANES), F32),
        scratch_shapes=[
            vmem(slots.shape, jnp.int32),
            vmem(geometry.shape, F32),
            vmem(mats.shape, F32),
            vmem((3, NODES * depth, LANES), F32),
            vmem(chi.shape, BF16),
            vmem(clo.shape, BF16),
            vmem((TALL, LANES), F32),
            vmem((4 * TALL, 2 * LANES), BF16),
            vmem((3 * depth // 2, 256, 2 * LANES), BF16),
            vmem((TALL * depth, LANES), F32),
            vmem(wire, F32),
            vmem(ends, F32),
            vmem((3, ROWS, depth, LANES), F32),
            vmem(ends, F32),
            vmem((wire[0] // 6, count // 8, 8) + wire[2:], F32),
            vmem((wire[0], count // 8, 8) + wire[2:], F32),
            vmem(single, F32),
            vmem(wire, F32),
            vmem(single, F32),
            vmem(wire, F32),
            vmem(ends, F32),
            vmem(face, F32),
            vmem(face, F32),
            vmem(face, F32),
            vmem(face, F32),
            vmem(end, F32),
            vmem(end, F32),
            vmem(end, F32),
            vmem(end, F32),
            dma((8,)),
            dma((1,)),
            dma((1,)),
            dma((5,)),
            dma((5,)),
            dma((5,)),
            dma((5,)),
            dma((7,)),
            dma((7,)),
            dma((4,)),
            dma((4,)),
            pltpu.SemaphoreType.REGULAR((4,)),
        ],
        compiler_params=pltpu.CompilerParams(collective_id=0, has_side_effects=True),
        name="step",
    )(slots, geometry, mats, chi, clo, velocity)


def body(velocity, slot_of_cell, elem_mats, geometry):
    depth = velocity.shape[1]
    table = coupling(depth * lax.axis_size("modes"))
    chi = np.asarray(table, np.float32).astype(jnp.bfloat16)
    clo = (table - chi.astype(np.float64)).astype(np.float32).astype(jnp.bfloat16)
    flat = jnp.swapaxes(velocity, 1, 2).reshape(3, NODES * depth, LANES)
    result = step(slot_of_cell, geometry, jnp.swapaxes(elem_mats, 0, 1), jnp.asarray(chi), jnp.asarray(clo), flat)
    return jnp.swapaxes(result, 1, 2)


def solution(mesh):
    in_specs = (P(None, "modes", None, "dom"), P("dom", None), P(), P(None, "dom"))
    out_specs = P(None, "modes", None, "dom")
    return jax.shard_map(body, mesh=mesh, in_specs=in_specs, out_specs=out_specs, check_vma=False)
```
